1024 devices in a mesh: lat: 32 (over x, y), lon: 8 (over z_hi, core), lev: 4 (over z_lo).
Axes of the slice: x: 4, y: 8, z: 16 (z_hi: 4, z_lo: 4; z = z_hi * 4 + z_lo), core: 2. Of those that a mesh axis runs over, the one named last changes fastest.
Arguments:
- adjoint_u: float32 [4, 512, 3600], P('lev', 'lat', 'lon'), may hold values from -6 to 6
- adjoint_v: float32 [4, 512, 3600], P('lev', 'lat', 'lon'), may hold values from -6 to 6
- adjoint_temp: float32 [4, 512, 3600], P('lev', 'lat', 'lon'), may hold values from -6 to 6
- adjoint_pres: float32 [512, 3600], P('lat', 'lon'), may hold values from -6 to 6
- carrying_eastward_flow: float32 [4, 512, 3600], P('lev', 'lat', 'lon'), may hold values from -4 to 4
- cutoff: int32 [2, 64], replicated, may hold values from 3 to 559, as said below
Outputs:
- prior_u: float32 [4, 512, 3600], P('lev', 'lat', 'lon')
- prior_v: float32 [4, 512, 3600], P('lev', 'lat', 'lon')
- prior_temp: float32 [4, 512, 3600], P('lev', 'lat', 'lon')
- prior_pres: float32 [512, 3600], P('lat', 'lon')
The draws below stay inside these ranges and needn't reach their ends.
Inputs may be any that keep to these rules, and one draw needn't show every extreme that they name: cutoff[h, r] belongs to the row r rows away from the south (h = 0) or north (h = 1) pole and lies between max(1, w // 2) and w - 1, with w = 2 + (5 * 3600 * (2 r + 1)) // 4096; both ends of the overall range are reached in every draw.
All inputs are finite; a program needn't handle non-finite values.
Results may differ from the reference program's by a relative error of at most 0.0002.
Values sent between devices are 32-bit elements; how exact they have to be, the bound alone decides.
A program may use at most 32 MiB of HBM per device.

```python
import jax
import jax.numpy as jnp
from jax import lax

NLON = 3600
NLEV = 4
NLAT = 512
POLAR = 64


def draw_cutoff(key, part):
    pole_rank = jnp.arange(POLAR, dtype=jnp.int32)
    upper = 2 + 5 * NLON * (2 * pole_rank + 1) // (8 * NLAT)
    lower = jnp.maximum(1, upper // 2)
    drawn = jax.random.randint(key, (2, POLAR), lower[None, :], upper[None, :], dtype=jnp.int32)
    drawn = drawn.at[0, POLAR - 1].set(upper[POLAR - 1] - 1)
    drawn = drawn.at[1, 0].set(lower[0])
    return drawn.astype(jnp.int32)


def levels(stream_key, dims, cuts, smallest, largest):
    gain, own = 1.0, jax.random.fold_in(stream_key, 6)
    for axis_at, blocks in cuts:
        steps = jnp.exp(jax.random.uniform(jax.random.fold_in(own, axis_at), (blocks,), jnp.float32, smallest / len(cuts), largest / len(cuts)))
        gain = gain * jnp.repeat(steps, dims[axis_at] // blocks).reshape([-1 if axis == axis_at else 1 for axis in range(len(dims))])
    return gain


def normal_values(stream_key, extent, spread, limit, cuts=(), held_as=jnp.bfloat16):
    array = spread * jax.random.normal(stream_key, extent, jnp.float32)
    if cuts:
        array = array * levels(stream_key, extent, cuts, -0.22, 0.18)
    return jnp.clip(array, -limit, limit).astype(held_as)


def setup_inputs(seed: int = 0) -> dict:
    streams_of = jax.random.split(jax.random.key(seed), 7)
    adjoint_u = normal_values(streams_of[0], (NLEV, NLAT, NLON), 1.0, 6.0, ((0, 4), (1, 32), (2, 8)), jnp.float32)
    adjoint_v = normal_values(streams_of[1], (NLEV, NLAT, NLON), 1.0, 6.0, ((0, 4), (1, 32), (2, 8)), jnp.float32)
    adjoint_temp = normal_values(streams_of[2], (NLEV, NLAT, NLON), 1.0, 6.0, ((0, 4), (1, 32), (2, 8)), jnp.float32)
    adjoint_pres = normal_values(streams_of[3], (NLAT, NLON), 1.0, 6.0, ((0, 32), (1, 8)), jnp.float32)
    carrying_eastward_flow = normal_values(streams_of[4], (NLEV, NLAT, NLON), 1.0, 4.0, ((0, 4), (1, 32), (2, 8)), jnp.float32)
    cutoff = draw_cutoff(jax.random.fold_in(streams_of[6], 71), 0)
    return {"adjoint_u": adjoint_u, "adjoint_v": adjoint_v, "adjoint_temp": adjoint_temp, "adjoint_pres": adjoint_pres, "carrying_eastward_flow": carrying_eastward_flow, "cutoff": cutoff}


zonal_courant = 0.15
merid_courant = 0.15
coriolis_scale = 0.4
heat_link_multiplier = 0.3

def eastward_grid_interval(values):
    return jnp.roll(values, -1, axis=-1) - jnp.roll(values, 1, axis=-1)

def merid_step(values, parity):
    half_turn = values.shape[-1] // 2
    south_ghost = parity * jnp.roll(values[..., :1, :], half_turn, axis=-1)
    north_ghost = parity * jnp.roll(values[..., -1:, :], half_turn, axis=-1)
    padded = jnp.concatenate([south_ghost, values, north_ghost], axis=-2)
    return padded[..., 2:, :] - padded[..., :-2, :]

def cutoff_rows(cutoff):
    row_index = jnp.arange(NLAT, dtype=jnp.int32)
    pole_rank = jnp.arange(POLAR, dtype=jnp.int32)
    south_cut = lax.optimization_barrier(jnp.sum(cutoff[0][None, :] * (row_index[:, None] == pole_rank[None, :]).astype(jnp.int32), axis=1))
    north_cut = lax.optimization_barrier(jnp.sum(cutoff[1][None, :] * (row_index[:, None] == NLAT - 1 - pole_rank[None, :]).astype(jnp.int32), axis=1))
    polar_row = (row_index < POLAR) | (row_index >= NLAT - POLAR)
    return jnp.where(polar_row, south_cut + north_cut, NLON).astype(jnp.int32)

def circle_spectral_damper(values, latitude_harmonic_limit):
    wave_numbers = jnp.arange(NLON // 2 + 1).astype(jnp.float32)[None, :]
    cut_float = latitude_harmonic_limit.astype(jnp.float32)[:, None]
    factor = jnp.where(wave_numbers <= cut_float, 1.0, (cut_float / jnp.maximum(wave_numbers, 1.0)) ** 2)
    spectrum = jnp.fft.rfft(values, axis=-1) * factor[None]
    return jnp.fft.irfft(spectrum, n=NLON, axis=-1)

def reference(adjoint_u, adjoint_v, adjoint_temp, adjoint_pres, carrying_eastward_flow, cutoff):
    latitude = ((jnp.arange(NLAT).astype(jnp.float32) + 0.5) / NLAT - 0.5) * jnp.pi
    eastward_scale_weight = (zonal_courant / jnp.cos(latitude))[:, None]
    coriolis = (coriolis_scale * jnp.sin(latitude))[:, None]
    latitude_harmonic_limit = cutoff_rows(cutoff)

    def linearized_update_map(eastward_flow_grid, northward_flow_grid, heat_state_grid, ground_barometric_grid):
        gravity_potential_level = heat_state_grid + ground_barometric_grid[None]
        eastward_flow_rate = coriolis * northward_flow_grid - eastward_scale_weight * eastward_grid_interval(gravity_potential_level)
        northward_flow_rate = -coriolis * eastward_flow_grid - merid_courant * merid_step(gravity_potential_level, 1.0)
        spreading_rate_grid = eastward_scale_weight * eastward_grid_interval(eastward_flow_grid) + merid_courant * merid_step(northward_flow_grid, -1.0)
        heat_change_rate = -eastward_scale_weight * carrying_eastward_flow * eastward_grid_interval(heat_state_grid) - heat_link_multiplier * spreading_rate_grid
        barometric_change_rate = -lax.optimization_barrier(jnp.sum(spreading_rate_grid, axis=0)) / NLEV
        return (eastward_flow_grid + circle_spectral_damper(eastward_flow_rate, latitude_harmonic_limit), northward_flow_grid + circle_spectral_damper(northward_flow_rate, latitude_harmonic_limit), heat_state_grid + circle_spectral_damper(heat_change_rate, latitude_harmonic_limit), ground_barometric_grid + barometric_change_rate)
    zero_field = jnp.zeros_like(adjoint_u)
    zero_plane = jnp.zeros_like(adjoint_pres)
    unused, pullback = jax.vjp(linearized_update_map, zero_field, zero_field, zero_field, zero_plane)
    prior_u, prior_v, prior_temp, prior_pres = pullback((adjoint_u, adjoint_v, adjoint_temp, adjoint_pres))
    return (prior_u, prior_v, prior_temp, prior_pres)
```

```python
import functools
import math

import jax
import jax.numpy as jnp
import ml_dtypes
import numpy as np
from jax import lax
from jax.experimental import pallas as pl
from jax.experimental.pallas import tpu as pltpu
from jax.sharding import PartitionSpec as P

zonal_courant = 0.15
merid_courant = 0.15
coriolis_scale = 0.4
heat_link_multiplier = 0.3

MESH = pl.DeviceIdType.MESH
PARTS = 8
ROOT_HALF = math.sqrt(0.5)


def lane_positions(width, padded):
    position = np.zeros(padded, np.int64)
    position[:width] = np.arange(width)
    position[width] = width
    position[padded - 1] = -1
    used = np.zeros(padded, bool)
    used[: width + 1] = True
    used[padded - 1] = True
    return position, used


def wave_tables(width, padded):
    position, used = lane_positions(width, padded)
    index = np.arange(padded)
    angle = 2.0 * np.pi * ((index[:, None] * position[None, :]) % width) / width
    live = (index < width)[:, None] & used[None, :]
    both = np.concatenate([np.where(live, np.cos(angle), 0.0), np.where(live, np.sin(angle), 0.0)], axis=1)
    high = both.astype(np.float32).astype(ml_dtypes.bfloat16)
    low = (both - high.astype(np.float64)).astype(np.float32).astype(ml_dtypes.bfloat16)
    residue = np.arange(8)
    twist = 2.0 * np.pi * ((residue[:, None] * position[None, :]) % (width * PARTS)) / (width * PARTS)
    twists = np.stack([np.cos(twist), np.sin(twist)]).astype(np.float32)
    return np.stack([high, low]), twists


def split(value):
    high = value.astype(jnp.bfloat16)
    return high, (value - high.astype(jnp.float32)).astype(jnp.bfloat16)


def wave_product(stack_ref, table_ref):
    rows = stack_ref.shape[0]
    high, low = split(stack_ref[...])
    lead = jnp.dot(jnp.concatenate([high, low], axis=0), table_ref[0], preferred_element_type=jnp.float32)
    rest = jnp.dot(high, table_ref[1], preferred_element_type=jnp.float32)
    return lead[:rows] + lead[rows:] + rest


def filter_blocks(blocks, result, stack, table, twists, cuts, width):
    rows, lanes = blocks.shape[1:]
    x = [blocks[d] for d in range(PARTS)]
    a = [x[d] + x[d + 4] for d in range(4)]
    b = [x[d] - x[d + 4] for d in range(4)]
    b_minus = (b[1] - b[3]) * ROOT_HALF
    b_plus = (b[1] + b[3]) * ROOT_HALF
    even, odd = a[0] + a[2], a[1] + a[3]
    waves = [
        (even + odd, None),
        (b[0] + b_minus, -b[2] - b_plus),
        (a[0] - a[2], a[3] - a[1]),
        (b[0] - b_minus, b[2] - b_plus),
        (even - odd, None),
    ]
    for r, (re, im) in enumerate(waves):
        if r == 0:
            new_re, new_im = re, jnp.zeros_like(re)
        else:
            c, s = twists[0, r : r + 1, :], twists[1, r : r + 1, :]
            new_re = re * c if im is None else re * c + im * s
            new_im = -re * s if im is None else im * c - re * s
        stack[8 * r : 8 * r + rows, :] = new_re
        stack[40 + 8 * r : 40 + 8 * r + rows, :] = new_im
    first = wave_product(stack, table)
    q = lax.broadcasted_iota(jnp.int32, (8, lanes), 1)
    row = lax.broadcasted_iota(jnp.int32, (8, lanes), 0)
    cut = jnp.where(lax.rem(row, 2) == 0, cuts[0], cuts[1])
    for r in range(5):
        wave = PARTS * q + r
        wave = jnp.minimum(wave, PARTS * width - wave).astype(jnp.float32)
        ratio = cut / jnp.maximum(wave, 1.0)
        weight = (1.0 if r in (0, 4) else 2.0) / (PARTS * width)
        factor = jnp.where(wave <= cut, 1.0, ratio * ratio) * weight
        factor = jnp.where(q < width, factor, 0.0)
        lo, hi = 8 * r, 40 + 8 * r
        re = first[lo : lo + 8, :lanes] + first[hi : hi + 8, lanes:]
        im = first[hi : hi + 8, :lanes] - first[lo : lo + 8, lanes:]
        stack[lo : lo + 8, :] = re * factor
        stack[hi : hi + 8, :] = im * factor
    second = wave_product(stack, table)
    back = []
    for r in range(5):
        lo, hi = 8 * r, 40 + 8 * r
        re = second[lo : lo + 8, :lanes] - second[hi : hi + 8, lanes:]
        if r == 0:
            back.append((re, None))
            continue
        im = second[hi : hi + 8, :lanes] + second[lo : lo + 8, lanes:]
        c, s = twists[0, r : r + 1, :], twists[1, r : r + 1, :]
        back.append((re * c - im * s, None if r == 4 else im * c + re * s))
    r0, r4 = back[0][0], back[4][0]
    (r1, i1), (r2, i2), (r3, i3) = back[1], back[2], back[3]
    plus, minus = r0 + r4, r0 - r4
    even_a, even_b = plus + r2, plus - r2
    odd_a, odd_b = minus - i2, minus + i2
    half = [
        r1 + r3,
        ((r1 - r3) - (i1 + i3)) * ROOT_HALF,
        i3 - i1,
        ((r3 - r1) - (i1 + i3)) * ROOT_HALF,
    ]
    base = [even_a, odd_a, even_b, odd_b]
    for d in range(4):
        result[d] = (base[d] + half[d])[:rows]
        result[d + 4] = (base[d] - half[d])[:rows]


def kernel(sizes, u_ref, v_ref, t_ref, p_ref, g_ref, cut_ref, table_hbm, twists,
           out_u, out_v, out_t, out_p,
           table, raw, pack, circles, stack, filtered, home, smooth,
           edge_out, edge_in, row_out, row_in, ghost, ext, height, heights,
           table_sem, edge_send, edge_recv, row_send, row_recv, circ_send, circ_recv,
           home_send, home_recv, ghost_send, ghost_recv, lev_send, lev_recv):
    lats, lons, levs, polar_ranks = sizes
    rows, width = p_ref.shape
    lanes = raw.shape[-1]
    lat, lon, lev = lax.axis_index("lat"), lax.axis_index("lon"), lax.axis_index("lev")
    polar_lat = lambda r: (r < polar_ranks) | (r >= lats - polar_ranks)
    polar = polar_lat(lat)
    across = lax.rem(lon + PARTS // 2, PARTS)
    south_filtered = (lat == 0) | polar_lat(lat - 1)
    north_filtered = (lat == lats - 1) | polar_lat(lat + 1)

    table_copy = pltpu.make_async_copy(table_hbm, table, table_sem)

    @pl.when(polar)
    def _():
        table_copy.start()

    barrier = pltpu.get_barrier_semaphore()

    def greet(**where):
        pl.semaphore_signal(barrier, inc=1, device_id=where, device_id_type=MESH)

    for k in range(1, PARTS):
        greet(lon=lax.rem(lon + k, PARTS))
    for k in range(1, levs):
        greet(lev=lax.rem(lev + k, levs))

    @pl.when(lat > 0)
    def _():
        greet(lat=lat - 1)

        @pl.when(south_filtered & (lon != PARTS - 1))
        def _():
            greet(lat=lat - 1, lon=PARTS - 1)

    @pl.when(lat < lats - 1)
    def _():
        greet(lat=lat + 1)

        @pl.when(north_filtered & (lon != 0))
        def _():
            greet(lat=lat + 1, lon=0)

    lane = lax.broadcasted_iota(jnp.int32, (rows, lanes), 1)
    last_tile = (width // 128) * 128
    for f, ref in enumerate((u_ref, v_ref, t_ref, g_ref, p_ref)):
        raw[f, :, last_tile:] = jnp.zeros((rows, lanes - last_tile), jnp.float32)
        raw[f, :, :width] = ref[...] if f == 4 else ref[0]
    raw_u, raw_v, raw_t, raw_g, raw_p = (raw[f] for f in range(5))
    small = lax.broadcasted_iota(jnp.int32, (rows, 128), 1)
    for side, column in ((0, 0), (1, width - 1)):
        edge = jnp.zeros((rows, 128), jnp.float32)
        for f, value in enumerate((raw_u, raw_t, raw_g, raw_p)):
            edge = jnp.where(small == f, value[:, column : column + 1], edge)
        edge_out[side] = edge
    for side, row in ((0, 0), (1, rows - 1)):
        for f, value in enumerate((raw_v, raw_t, raw_p)):
            row_out[side, f : f + 1, :] = value[row : row + 1]

    @pl.when(polar)
    def _():
        for e in range(PARTS):
            for f, value in enumerate((raw_u, raw_v, raw_t)):
                pack[e, 2 * f : 2 * f + 2, :] = value[2 * e : 2 * e + 2]

    count = lambda condition: jnp.where(condition, 1, 0)
    below, above = lat > 0, lat < lats - 1
    arrivals = PARTS - 1 + levs - 1 + count(below) + count(above)
    arrivals += (PARTS - 1) * count(polar & ((below & (lon == 0)) | (above & (lon == PARTS - 1))))
    pl.semaphore_wait(barrier, arrivals)

    def send(src, dst, send_sem, recv_sem, **where):
        return pltpu.make_async_remote_copy(
            src_ref=src, dst_ref=dst, send_sem=send_sem, recv_sem=recv_sem,
            device_id=where, device_id_type=MESH)

    circ_copies = [
        send(pack.at[lax.rem(lon + k, PARTS)], circles.at[lon], circ_send.at[k], circ_recv.at[k],
             lon=lax.rem(lon + k, PARTS))
        for k in range(1, PARTS)
    ]

    @pl.when(polar)
    def _():
        for k in (4, 3, 5, 2, 6, 1, 7):
            circ_copies[k - 1].start()

    edge_copies = [
        send(edge_out.at[0], edge_in.at[0], edge_send.at[0], edge_recv.at[0], lon=lax.rem(lon + PARTS - 1, PARTS)),
        send(edge_out.at[1], edge_in.at[1], edge_send.at[1], edge_recv.at[1], lon=lax.rem(lon + 1, PARTS)),
    ]
    for copy in edge_copies:
        copy.start()

    @pl.when(lat > 0)
    def _():
        send(row_out.at[0], row_in.at[1], row_send.at[0], row_recv.at[1], lat=lat - 1).start()

    @pl.when(lat == 0)
    def _():
        send(row_out.at[0], row_in.at[0], row_send.at[0], row_recv.at[0], lon=across).start()

    @pl.when(lat < lats - 1)
    def _():
        send(row_out.at[1], row_in.at[0], row_send.at[1], row_recv.at[0], lat=lat + 1).start()

    @pl.when(lat == lats - 1)
    def _():
        send(row_out.at[1], row_in.at[1], row_send.at[1], row_recv.at[1], lon=across).start()

    @pl.when(polar)
    def _():
        own = jnp.where(lat < polar_ranks, 0, 1)
        row = lat * rows + 2 * lon
        cuts = []
        for j in range(2):
            rank = jnp.where(own == 0, row + j, lats * rows - 1 - (row + j))
            cuts.append(cut_ref[own, rank].astype(jnp.float32))
        circles[lon] = pack[lon]
        table_copy.wait()
        for k in range(1, PARTS):
            circ_copies[k - 1].wait_recv()
        filter_blocks(circles, filtered, stack, table, twists, cuts, width)

    home_copies = [
        send(filtered.at[lax.rem(lon + k, PARTS)], home.at[lon], home_send.at[k], home_recv.at[k],
             lon=lax.rem(lon + k, PARTS))
        for k in range(1, PARTS)
    ]

    def ghost_copy(d, side, **where):
        return send(filtered.at[d], ghost.at[side], ghost_send.at[d], ghost_recv.at[side], **where)

    def ghost_copies(act):
        @pl.when(polar & (lon == 0))
        def _():
            for d in range(PARTS):
                @pl.when(lat > 0)
                def _():
                    act(ghost_copy(d, 1, lat=lat - 1, lon=d))

                if d != PARTS // 2:
                    @pl.when(lat == 0)
                    def _():
                        act(ghost_copy(d, 0, lon=(d + PARTS // 2) % PARTS))

        @pl.when(polar & (lon == PARTS - 1))
        def _():
            for d in range(PARTS):
                @pl.when(lat < lats - 1)
                def _():
                    act(ghost_copy(d, 0, lat=lat + 1, lon=d))

                if d != PARTS // 2 - 1:
                    @pl.when(lat == lats - 1)
                    def _():
                        act(ghost_copy(d, 1, lon=(d + PARTS // 2) % PARTS))

    self_south = (lat == 0) & (lon == 0)
    self_north = (lat == lats - 1) & (lon == PARTS - 1)

    @pl.when(polar)
    def _():
        for k in (4, 3, 5, 2, 6, 1, 7):
            home_copies[k - 1].start()

    ghost_copies(lambda copy: copy.start())

    @pl.when(self_south)
    def _():
        ghost[0] = filtered[PARTS // 2]

    @pl.when(self_north)
    def _():
        ghost[1] = filtered[PARTS // 2 - 1]

    for copy in edge_copies:
        copy.wait_recv()
    for side in range(2):
        pltpu.make_async_copy(row_out.at[side], row_in.at[side], row_recv.at[side]).wait()

    def with_edges(value, f):
        east, west = edge_in[0][:, f : f + 1], edge_in[1][:, f : f + 1]
        return jnp.where(lane == width, east, jnp.where(lane == lanes - 1, west, value))

    flow, pres = with_edges(raw_g, 2), with_edges(raw_p, 3)

    @pl.when(jnp.logical_not(polar))
    def _():
        smooth[0] = with_edges(raw_u, 0)
        smooth[1] = raw_v
        smooth[2] = with_edges(raw_t, 1)

    latitude = (lat * rows + lax.broadcasted_iota(jnp.int32, (rows, 128), 0)).astype(jnp.float32)
    latitude = ((latitude + 0.5) / (lats * rows) - 0.5) * jnp.float32(math.pi)
    scale = (zonal_courant / jnp.cos(latitude))[:, :1]
    coriolis = (coriolis_scale * jnp.sin(latitude))[:, :1]

    @pl.when(polar)
    def _():
        home[lon] = filtered[lon]
        for k in range(1, PARTS):
            home_copies[k - 1].wait_recv()
        for e in range(PARTS):
            for f in range(3):
                smooth[f, 2 * e : 2 * e + 2, :] = home[e, 2 * f : 2 * f + 2, :]

    @pl.when(south_filtered & jnp.logical_not(self_south))
    def _():
        pltpu.make_async_copy(filtered.at[0], ghost.at[0], ghost_recv.at[0]).wait()

    @pl.when(north_filtered & jnp.logical_not(self_north))
    def _():
        pltpu.make_async_copy(filtered.at[0], ghost.at[1], ghost_recv.at[1]).wait()

    def zonal(value):
        return pltpu.roll(value, lanes - 1, 1) - pltpu.roll(value, 1, 1)

    fu, fv, ft = smooth[0], smooth[1], smooth[2]
    div = -heat_link_multiplier * ft - pres * (1.0 / levs)
    ext[0, 8 : 8 + rows, :] = fv
    ext[1, 8 : 8 + rows, :] = div
    for side, at in ((0, 7), (1, 8 + rows)):
        wanted = south_filtered if side == 0 else north_filtered
        pole = (lat == 0) if side == 0 else (lat == lats - 1)
        upper = jnp.where(pole, side == 1, side == 0)
        g = ghost[side]
        gv = jnp.where(upper, g[3:4], g[2:3])
        gt = jnp.where(upper, g[5:6], g[4:5])
        gv = jnp.where(wanted, gv, row_in[side, 0:1, :])
        gt = jnp.where(wanted, gt, row_in[side, 1:2, :])
        gp = row_in[side, 2:3, :]
        ext[0, at : at + 1, :] = jnp.where(pole, -gv, gv)
        ext[1, at : at + 1, :] = -heat_link_multiplier * gt - gp * (1.0 / levs)
    merid_v = ext[0, 9 : 9 + rows, :] - ext[0, 7 : 7 + rows, :]
    merid_div = ext[1, 9 : 9 + rows, :] - ext[1, 7 : 7 + rows, :]
    bar = scale * zonal(fu) + merid_courant * merid_v
    height[...] = bar
    lev_copies = [
        send(height, heights.at[k], lev_send.at[k], lev_recv.at[k], lev=lax.rem(lev + k, levs))
        for k in range(1, levs)
    ]
    for copy in lev_copies:
        copy.start()
    out_u[0] = (raw_u - coriolis * fv - scale * zonal(div))[:, :width]
    out_v[0] = (raw_v + coriolis * fu - merid_courant * merid_div)[:, :width]
    out_t[0] = (raw_t + bar + scale * zonal(flow * ft))[:, :width]

    for copy in edge_copies:
        copy.wait_send()
    for side in range(2):
        pltpu.make_async_copy(row_out.at[side], row_in.at[side], row_send.at[side]).wait()

    @pl.when(polar)
    def _():
        for copy in circ_copies:
            copy.wait_send()
        for copy in home_copies:
            copy.wait_send()

    ghost_copies(lambda copy: copy.wait_send())
    total = raw_p + bar
    for copy in lev_copies:
        copy.wait_recv()
    for k in range(1, levs):
        total = total + heights[k]
    out_p[...] = total[:, :width]
    for copy in lev_copies:
        copy.wait_send()


def solution(mesh):
    lats, lons, levs = mesh.shape["lat"], mesh.shape["lon"], mesh.shape["lev"]
    field, plane = P("lev", "lat", "lon"), P("lat", "lon")

    def local(adjoint_u, adjoint_v, adjoint_temp, adjoint_pres, carrying_eastward_flow, cutoff):
        rows, width = adjoint_pres.shape
        lanes = (width + 2 + 127) // 128 * 128
        table, twists = wave_tables(width, lanes)
        sizes = (lats, lons, levs, cutoff.shape[1] // rows)
        vmem = pl.BlockSpec(memory_space=pltpu.VMEM)
        f32, dma = jnp.float32, pltpu.SemaphoreType.DMA
        block = (PARTS, 6, lanes)
        return pl.pallas_call(
            functools.partial(kernel, sizes),
            name="adjoint_step",
            out_shape=[jax.ShapeDtypeStruct(adjoint_u.shape, f32)] * 3
            + [jax.ShapeDtypeStruct(adjoint_pres.shape, f32)],
            in_specs=[vmem] * 5
            + [pl.BlockSpec(memory_space=pltpu.SMEM), pl.BlockSpec(memory_space=pl.ANY), vmem],
            out_specs=[vmem] * 4,
            scratch_shapes=[
                pltpu.VMEM(table.shape, jnp.bfloat16),
                pltpu.VMEM((5, rows, lanes), f32),
                pltpu.VMEM(block, f32),
                pltpu.VMEM(block, f32),
                pltpu.VMEM((80, lanes), f32),
                pltpu.VMEM(block, f32),
                pltpu.VMEM(block, f32),
                pltpu.VMEM((3, rows, lanes), f32),
                pltpu.VMEM((2, rows, 128), f32),
                pltpu.VMEM((2, rows, 128), f32),
                pltpu.VMEM((2, 3, lanes), f32),
                pltpu.VMEM((2, 3, lanes), f32),
                pltpu.VMEM((2, 6, lanes), f32),
                pltpu.VMEM((2, rows + 16, lanes), f32),
                pltpu.VMEM((rows, lanes), f32),
                pltpu.VMEM((levs, rows, lanes), f32),
                dma, dma((2,)), dma((2,)), dma((2,)), dma((2,)),
                dma((PARTS,)), dma((PARTS,)), dma((PARTS,)), dma((PARTS,)),
                dma((PARTS,)), dma((2,)), dma((levs,)), dma((levs,)),
            ],
            compiler_params=pltpu.CompilerParams(collective_id=0, has_side_effects=True),
        )(adjoint_u, adjoint_v, adjoint_temp, adjoint_pres, carrying_eastward_flow, cutoff,
          jnp.asarray(table), jnp.asarray(twists))

    return jax.shard_map(
        local, mesh=mesh, in_specs=(field, field, field, plane, field, P()),
        out_specs=(field, field, field, plane), check_vma=False)
```

```python
import functools
import math

import jax
import jax.numpy as jnp
import ml_dtypes
import numpy as np
from jax import lax
from jax.experimental import pallas as pl
from jax.experimental.pallas import tpu as pltpu
from jax.sharding import PartitionSpec as P

zonal_courant = 0.15
merid_courant = 0.15
coriolis_scale = 0.4
heat_link_multiplier = 0.3

MESH = pl.DeviceIdType.MESH
PARTS = 8
ROOT_HALF = math.sqrt(0.5)


def lane_positions(width, padded):
    position = np.zeros(padded, np.int64)
    position[:width] = np.arange(width)
    position[width] = width
    position[padded - 1] = -1
    used = np.zeros(padded, bool)
    used[: width + 1] = True
    used[padded - 1] = True
    return position, used


def wave_tables(width, padded):
    position, used = lane_positions(width, padded)
    index = np.arange(padded)
    angle = 2.0 * np.pi * ((index[:, None] * position[None, :]) % width) / width
    live = (index < width)[:, None] & used[None, :]
    both = np.concatenate([np.where(live, np.cos(angle), 0.0), np.where(live, np.sin(angle), 0.0)], axis=1)
    high = both.astype(np.float32).astype(ml_dtypes.bfloat16)
    low = (both - high.astype(np.float64)).astype(np.float32).astype(ml_dtypes.bfloat16)
    residue = np.arange(8)
    twist = 2.0 * np.pi * ((residue[:, None] * position[None, :]) % (width * PARTS)) / (width * PARTS)
    twists = np.stack([np.cos(twist), np.sin(twist)]).astype(np.float32)
    return np.stack([high, low]), twists


def split(value):
    high = value.astype(jnp.bfloat16)
    return high, (value - high.astype(jnp.float32)).astype(jnp.bfloat16)


def wave_product(stack_ref, table_ref):
    rows = stack_ref.shape[0]
    high, low = split(stack_ref[...])
    lead = jnp.dot(jnp.concatenate([high, low], axis=0), table_ref[0], preferred_element_type=jnp.float32)
    rest = jnp.dot(high, table_ref[1], preferred_element_type=jnp.float32)
    return lead[:rows] + lead[rows:] + rest


def filter_blocks(blocks, result, stack, table, twists, cuts, width):
    rows, lanes = blocks.shape[1:]
    x = [blocks[d] for d in range(PARTS)]
    a = [x[d] + x[d + 4] for d in range(4)]
    b = [x[d] - x[d + 4] for d in range(4)]
    b_minus = (b[1] - b[3]) * ROOT_HALF
    b_plus = (b[1] + b[3]) * ROOT_HALF
    even, odd = a[0] + a[2], a[1] + a[3]
    waves = [
        (even + odd, None),
        (b[0] + b_minus, -b[2] - b_plus),
        (a[0] - a[2], a[3] - a[1]),
        (b[0] - b_minus, b[2] - b_plus),
        (even - odd, None),
    ]
    for r, (re, im) in enumerate(waves):
        if r == 0:
            new_re, new_im = re, jnp.zeros_like(re)
        else:
            c, s = twists[0, r : r + 1, :], twists[1, r : r + 1, :]
            new_re = re * c if im is None else re * c + im * s
            new_im = -re * s if im is None else im * c - re * s
        stack[8 * r : 8 * r + rows, :] = new_re
        stack[40 + 8 * r : 40 + 8 * r + rows, :] = new_im
    first = wave_product(stack, table)
    q = lax.broadcasted_iota(jnp.int32, (8, lanes), 1)
    row = lax.broadcasted_iota(jnp.int32, (8, lanes), 0)
    cut = jnp.where(lax.rem(row, 2) == 0, cuts[0], cuts[1])
    for r in range(5):
        wave = PARTS * q + r
        wave = jnp.minimum(wave, PARTS * width - wave).astype(jnp.float32)
        ratio = cut / jnp.maximum(wave, 1.0)
        weight = (1.0 if r in (0, 4) else 2.0) / (PARTS * width)
        factor = jnp.where(wave <= cut, 1.0, ratio * ratio) * weight
        factor = jnp.where(q < width, factor, 0.0)
        lo, hi = 8 * r, 40 + 8 * r
        re = first[lo : lo + 8, :lanes] + first[hi : hi + 8, lanes:]
        im = first[hi : hi + 8, :lanes] - first[lo : lo + 8, lanes:]
        stack[lo : lo + 8, :] = re * factor
        stack[hi : hi + 8, :] = im * factor
    second = wave_product(stack, table)
    back = []
    for r in range(5):
        lo, hi = 8 * r, 40 + 8 * r
        re = second[lo : lo + 8, :lanes] - second[hi : hi + 8, lanes:]
        if r == 0:
            back.append((re, None))
            continue
        im = second[hi : hi + 8, :lanes] + second[lo : lo + 8, lanes:]
        c, s = twists[0, r : r + 1, :], twists[1, r : r + 1, :]
        back.append((re * c - im * s, None if r == 4 else im * c + re * s))
    r0, r4 = back[0][0], back[4][0]
    (r1, i1), (r2, i2), (r3, i3) = back[1], back[2], back[3]
    plus, minus = r0 + r4, r0 - r4
    even_a, even_b = plus + r2, plus - r2
    odd_a, odd_b = minus - i2, minus + i2
    half = [
        r1 + r3,
        ((r1 - r3) - (i1 + i3)) * ROOT_HALF,
        i3 - i1,
        ((r3 - r1) - (i1 + i3)) * ROOT_HALF,
    ]
    base = [even_a, odd_a, even_b, odd_b]
    for d in range(4):
        result[d] = (base[d] + half[d])[:rows]
        result[d + 4] = (base[d] - half[d])[:rows]


def kernel(sizes, u_hbm, v_hbm, t_hbm, p_hbm, g_hbm, cut_ref, table_hbm, twists_hbm, packed,
           u_ref, v_ref, t_ref, p_ref, g_ref, twists, table, raw, pack, circles, stack, filtered, home, smooth,
           edge_out, edge_in, row_out, row_in, ghost_out, ghost, ext, height, heights,
           input_sem, table_sem, edge_send, edge_recv, row_send, row_recv, circ_send, circ_recv,
           home_send, home_recv, ghost_send, ghost_recv, lev_send, lev_recv):
    lats, lons, levs, polar_ranks = sizes
    rows, width = p_ref.shape
    lanes = raw.shape[-1]
    lat, lon, lev = lax.axis_index("lat"), lax.axis_index("lon"), lax.axis_index("lev")
    polar_lat = lambda r: (r < polar_ranks) | (r >= lats - polar_ranks)
    polar = polar_lat(lat)
    across = lax.rem(lon + PARTS // 2, PARTS)
    south_filtered = (lat == 0) | polar_lat(lat - 1)
    north_filtered = (lat == lats - 1) | polar_lat(lat + 1)

    barrier = pltpu.get_barrier_semaphore()

    def greet(**where):
        pl.semaphore_signal(barrier, inc=1, device_id=where, device_id_type=MESH)

    for k in range(1, PARTS):
        greet(lon=lax.rem(lon + k, PARTS))
    for k in range(1, levs):
        greet(lev=lax.rem(lev + k, levs))

    @pl.when(lat > 0)
    def _():
        greet(lat=lat - 1)

        @pl.when(south_filtered & (lon != PARTS - 1))
        def _():
            greet(lat=lat - 1, lon=PARTS - 1)

    @pl.when(lat < lats - 1)
    def _():
        greet(lat=lat + 1)

        @pl.when(north_filtered & (lon != 0))
        def _():
            greet(lat=lat + 1, lon=0)

    input_copies = [
        pltpu.make_async_copy(src, dst, input_sem.at[k])
        for k, (src, dst) in enumerate(
            ((u_hbm, u_ref), (v_hbm, v_ref), (t_hbm, t_ref), (g_hbm, g_ref), (p_hbm, p_ref)))
    ]
    table_copies = [
        pltpu.make_async_copy(twists_hbm, twists, table_sem.at[0]),
        pltpu.make_async_copy(table_hbm, table, table_sem.at[1]),
    ]
    for copy in input_copies:
        copy.start()

    @pl.when(polar)
    def _():
        for copy in table_copies:
            copy.start()

    lane = lax.broadcasted_iota(jnp.int32, (rows, lanes), 1)
    last_tile = (width // 128) * 128
    for f, ref in enumerate((u_ref, v_ref, t_ref, g_ref, p_ref)):
        input_copies[f].wait()
        raw[f, :, last_tile:] = jnp.zeros((rows, lanes - last_tile), jnp.float32)
        raw[f, :, :width] = ref[...] if f == 4 else ref[0]
    raw_u, raw_v, raw_t, raw_g, raw_p = (raw[f] for f in range(5))
    small = lax.broadcasted_iota(jnp.int32, (rows, 128), 1)
    for side, column in ((0, 0), (1, width - 1)):
        edge = jnp.zeros((rows, 128), jnp.float32)
        for f, value in enumerate((raw_u, raw_t, raw_g, raw_p)):
            edge = jnp.where(small == f, value[:, column : column + 1], edge)
        edge_out[side] = edge
    for side, row in ((0, 0), (1, rows - 1)):
        for f, value in enumerate((raw_v, raw_t, raw_p)):
            row_out[side, f : f + 1, :] = value[row : row + 1]

    @pl.when(polar)
    def _():
        for e in range(PARTS):
            for f, value in enumerate((raw_u, raw_v, raw_t)):
                pack[e, 2 * f : 2 * f + 2, :] = value[2 * e : 2 * e + 2]

    count = lambda condition: jnp.where(condition, 1, 0)
    below, above = lat > 0, lat < lats - 1
    arrivals = PARTS - 1 + levs - 1 + count(below) + count(above)
    arrivals += (PARTS - 1) * count(polar & ((below & (lon == 0)) | (above & (lon == PARTS - 1))))
    pl.semaphore_wait(barrier, arrivals)

    def send(src, dst, send_sem, recv_sem, **where):
        return pltpu.make_async_remote_copy(
            src_ref=src, dst_ref=dst, send_sem=send_sem, recv_sem=recv_sem,
            device_id=where, device_id_type=MESH)

    circ_copies = [
        send(pack.at[lax.rem(lon + k, PARTS)], circles.at[lon], circ_send.at[k], circ_recv.at[k],
             lon=lax.rem(lon + k, PARTS))
        for k in range(1, PARTS)
    ]

    @pl.when(polar)
    def _():
        for k in (4, 3, 5, 2, 6, 1, 7):
            circ_copies[k - 1].start()

    edge_copies = [
        send(edge_out.at[0], edge_in.at[0], edge_send.at[0], edge_recv.at[0], lon=lax.rem(lon + PARTS - 1, PARTS)),
        send(edge_out.at[1], edge_in.at[1], edge_send.at[1], edge_recv.at[1], lon=lax.rem(lon + 1, PARTS)),
    ]
    for copy in edge_copies:
        copy.start()

    @pl.when(lat > 0)
    def _():
        send(row_out.at[0], row_in.at[1], row_send.at[0], row_recv.at[1], lat=lat - 1).start()

    @pl.when(lat == 0)
    def _():
        send(row_out.at[0], row_in.at[0], row_send.at[0], row_recv.at[0], lon=across).start()

    @pl.when(lat < lats - 1)
    def _():
        send(row_out.at[1], row_in.at[0], row_send.at[1], row_recv.at[0], lat=lat + 1).start()

    @pl.when(lat == lats - 1)
    def _():
        send(row_out.at[1], row_in.at[1], row_send.at[1], row_recv.at[1], lon=across).start()

    @pl.when(polar)
    def _():
        own = jnp.where(lat < polar_ranks, 0, 1)
        row = lat * rows + 2 * lon
        cuts = []
        for j in range(2):
            rank = jnp.where(own == 0, row + j, lats * rows - 1 - (row + j))
            cuts.append(cut_ref[own, rank].astype(jnp.float32))
        circles[lon] = pack[lon]
        for copy in table_copies:
            copy.wait()
        for k in range(1, PARTS):
            circ_copies[k - 1].wait_recv()
        filter_blocks(circles, filtered, stack, table, twists, cuts, width)

    home_copies = [
        send(filtered.at[lax.rem(lon + k, PARTS)], home.at[lon], home_send.at[k], home_recv.at[k],
             lon=lax.rem(lon + k, PARTS))
        for k in range(1, PARTS)
    ]

    def ghost_copy(d, side, **where):
        return send(ghost_out.at[d], ghost.at[side], ghost_send.at[d], ghost_recv.at[side], **where)

    def ghost_copies(act):
        @pl.when(polar & (lon == 0))
        def _():
            for d in range(PARTS):
                @pl.when(lat > 0)
                def _():
                    act(ghost_copy(d, 1, lat=lat - 1, lon=d))

                if d != PARTS // 2:
                    @pl.when(lat == 0)
                    def _():
                        act(ghost_copy(d, 0, lon=(d + PARTS // 2) % PARTS))

        @pl.when(polar & (lon == PARTS - 1))
        def _():
            for d in range(PARTS):
                @pl.when(lat < lats - 1)
                def _():
                    act(ghost_copy(d, 0, lat=lat + 1, lon=d))

                if d != PARTS // 2 - 1:
                    @pl.when(lat == lats - 1)
                    def _():
                        act(ghost_copy(d, 1, lon=(d + PARTS // 2) % PARTS))

    @pl.when(polar & (lon == 0))
    def _():
        for d in range(PARTS):
            ghost_out[d, 0:1, :] = filtered[d, 2:3, :]
            ghost_out[d, 1:2, :] = filtered[d, 4:5, :]

    @pl.when(polar & (lon == PARTS - 1))
    def _():
        for d in range(PARTS):
            ghost_out[d, 0:1, :] = filtered[d, 3:4, :]
            ghost_out[d, 1:2, :] = filtered[d, 5:6, :]

    self_south = (lat == 0) & (lon == 0)
    self_north = (lat == lats - 1) & (lon == PARTS - 1)

    @pl.when(polar)
    def _():
        for k in (4, 3, 5, 2, 6, 1, 7):
            home_copies[k - 1].start()

    ghost_copies(lambda copy: copy.start())

    @pl.when(self_south)
    def _():
        ghost[0] = ghost_out[PARTS // 2]

    @pl.when(self_north)
    def _():
        ghost[1] = ghost_out[PARTS // 2 - 1]

    for copy in edge_copies:
        copy.wait_recv()
    for side in range(2):
        pltpu.make_async_copy(row_out.at[side], row_in.at[side], row_recv.at[side]).wait()

    def with_edges(value, f):
        east, west = edge_in[0][:, f : f + 1], edge_in[1][:, f : f + 1]
        return jnp.where(lane == width, east, jnp.where(lane == lanes - 1, west, value))

    flow, pres = with_edges(raw_g, 2), with_edges(raw_p, 3)

    @pl.when(jnp.logical_not(polar))
    def _():
        smooth[0] = with_edges(raw_u, 0)
        smooth[1] = raw_v
        smooth[2] = with_edges(raw_t, 1)

    latitude = (lat * rows + lax.broadcasted_iota(jnp.int32, (rows, 128), 0)).astype(jnp.float32)
    latitude = ((latitude + 0.5) / (lats * rows) - 0.5) * jnp.float32(math.pi)
    scale = (zonal_courant / jnp.cos(latitude))[:, :1]
    coriolis = (coriolis_scale * jnp.sin(latitude))[:, :1]

    @pl.when(polar)
    def _():
        home[lon] = filtered[lon]
        for k in range(1, PARTS):
            home_copies[k - 1].wait_recv()
        for e in range(PARTS):
            for f in range(3):
                smooth[f, 2 * e : 2 * e + 2, :] = home[e, 2 * f : 2 * f + 2, :]

    @pl.when(south_filtered & jnp.logical_not(self_south))
    def _():
        pltpu.make_async_copy(ghost_out.at[0], ghost.at[0], ghost_recv.at[0]).wait()

    @pl.when(north_filtered & jnp.logical_not(self_north))
    def _():
        pltpu.make_async_copy(ghost_out.at[0], ghost.at[1], ghost_recv.at[1]).wait()

    def zonal(value):
        return pltpu.roll(value, lanes - 1, 1) - pltpu.roll(value, 1, 1)

    fu, fv, ft = smooth[0], smooth[1], smooth[2]
    div = -heat_link_multiplier * ft - pres * (1.0 / levs)
    ext[0, 8 : 8 + rows, :] = fv
    ext[1, 8 : 8 + rows, :] = div
    for side, at in ((0, 7), (1, 8 + rows)):
        wanted = south_filtered if side == 0 else north_filtered
        pole = (lat == 0) if side == 0 else (lat == lats - 1)
        gv = jnp.where(wanted, ghost[side, 0:1, :], row_in[side, 0:1, :])
        gt = jnp.where(wanted, ghost[side, 1:2, :], row_in[side, 1:2, :])
        gp = row_in[side, 2:3, :]
        ext[0, at : at + 1, :] = jnp.where(pole, -gv, gv)
        ext[1, at : at + 1, :] = -heat_link_multiplier * gt - gp * (1.0 / levs)
    merid_v = ext[0, 9 : 9 + rows, :] - ext[0, 7 : 7 + rows, :]
    merid_div = ext[1, 9 : 9 + rows, :] - ext[1, 7 : 7 + rows, :]
    bar = scale * zonal(fu) + merid_courant * merid_v
    height[...] = bar
    lev_copies = [
        send(height, heights.at[k], lev_send.at[k], lev_recv.at[k], lev=lax.rem(lev + k, levs))
        for k in range(1, levs)
    ]
    for copy in lev_copies:
        copy.start()
    packed[0] = (raw_u - coriolis * fv - scale * zonal(div))
    packed[1] = (raw_v + coriolis * fu - merid_courant * merid_div)
    packed[2] = (raw_t + bar + scale * zonal(flow * ft))

    for copy in edge_copies:
        copy.wait_send()
    for side in range(2):
        pltpu.make_async_copy(row_out.at[side], row_in.at[side], row_send.at[side]).wait()

    @pl.when(polar)
    def _():
        for copy in circ_copies:
            copy.wait_send()
        for copy in home_copies:
            copy.wait_send()

    ghost_copies(lambda copy: copy.wait_send())
    total = raw_p + bar
    for copy in lev_copies:
        copy.wait_recv()
    for k in range(1, levs):
        total = total + heights[k]
    packed[3] = total
    for copy in lev_copies:
        copy.wait_send()


def unpack(packed, out_u, out_v, out_t, out_p):
    width = out_p.shape[-1]
    out_u[0] = packed[0, :, :width]
    out_v[0] = packed[1, :, :width]
    out_t[0] = packed[2, :, :width]
    out_p[...] = packed[3, :, :width]


def solution(mesh):
    lats, lons, levs = mesh.shape["lat"], mesh.shape["lon"], mesh.shape["lev"]
    field, plane = P("lev", "lat", "lon"), P("lat", "lon")

    def local(adjoint_u, adjoint_v, adjoint_temp, adjoint_pres, carrying_eastward_flow, cutoff):
        rows, width = adjoint_pres.shape
        lanes = (width + 2 + 127) // 128 * 128
        table, twists = wave_tables(width, lanes)
        sizes = (lats, lons, levs, cutoff.shape[1] // rows)
        vmem = pl.BlockSpec(memory_space=pltpu.VMEM)
        anywhere = pl.BlockSpec(memory_space=pl.ANY)
        f32, dma = jnp.float32, pltpu.SemaphoreType.DMA
        block = (PARTS, 6, lanes)
        packed = pl.pallas_call(
            functools.partial(kernel, sizes),
            name="adjoint_step",
            out_shape=jax.ShapeDtypeStruct((4, rows, lanes), f32),
            in_specs=[anywhere] * 5 + [pl.BlockSpec(memory_space=pltpu.SMEM)] + [anywhere] * 2,
            out_specs=vmem,
            scratch_shapes=[
                pltpu.VMEM((1, rows, width), f32),
                pltpu.VMEM((1, rows, width), f32),
                pltpu.VMEM((1, rows, width), f32),
                pltpu.VMEM((rows, width), f32),
                pltpu.VMEM((1, rows, width), f32),
                pltpu.VMEM(twists.shape, f32),
                pltpu.VMEM(table.shape, jnp.bfloat16),
                pltpu.VMEM((5, rows, lanes), f32),
                pltpu.VMEM(block, f32),
                pltpu.VMEM(block, f32),
                pltpu.VMEM((80, lanes), f32),
                pltpu.VMEM(block, f32),
                pltpu.VMEM(block, f32),
                pltpu.VMEM((3, rows, lanes), f32),
                pltpu.VMEM((2, rows, 128), f32),
                pltpu.VMEM((2, rows, 128), f32),
                pltpu.VMEM((2, 3, lanes), f32),
                pltpu.VMEM((2, 3, lanes), f32),
                pltpu.VMEM((PARTS, 2, lanes), f32),
                pltpu.VMEM((2, 2, lanes), f32),
                pltpu.VMEM((2, rows + 16, lanes), f32),
                pltpu.VMEM((rows, lanes), f32),
                pltpu.VMEM((levs, rows, lanes), f32),
                dma((5,)), dma((2,)), dma((2,)), dma((2,)), dma((2,)), dma((2,)),
                dma((PARTS,)), dma((PARTS,)), dma((PARTS,)), dma((PARTS,)),
                dma((PARTS,)), dma((2,)), dma((levs,)), dma((levs,)),
            ],
            compiler_params=pltpu.CompilerParams(collective_id=0, has_side_effects=True),
        )(adjoint_u, adjoint_v, adjoint_temp, adjoint_pres, carrying_eastward_flow, cutoff,
          jnp.asarray(table), jnp.asarray(twists))
        return pl.pallas_call(
            unpack,
            name="hand_on",
            out_shape=[jax.ShapeDtypeStruct(adjoint_u.shape, f32)] * 3
            + [jax.ShapeDtypeStruct(adjoint_pres.shape, f32)],
            in_specs=[vmem],
            out_specs=[vmem] * 4,
        )(packed)

    return jax.shard_map(
        local, mesh=mesh, in_specs=(field, field, field, plane, field, P()),
        out_specs=(field, field, field, plane), check_vma=False)
```

```python
import functools
import math

import jax
import jax.numpy as jnp
import ml_dtypes
import numpy as np
from jax import lax
from jax.experimental import pallas as pl
from jax.experimental.pallas import tpu as pltpu
from jax.sharding import PartitionSpec as P

zonal_courant = 0.15
merid_courant = 0.15
coriolis_scale = 0.4
heat_link_multiplier = 0.3

MESH = pl.DeviceIdType.MESH
PARTS = 8
ROOT_HALF = math.sqrt(0.5)


def lane_positions(width, padded):
    position = np.zeros(padded, np.int64)
    position[:width] = np.arange(width)
    position[width] = width
    position[padded - 1] = -1
    used = np.zeros(padded, bool)
    used[: width + 1] = True
    used[padded - 1] = True
    return position, used


def wave_tables(width, padded):
    position, used = lane_positions(width, padded)
    index = np.arange(padded)
    angle = 2.0 * np.pi * ((index[:, None] * position[None, :]) % width) / width
    live = (index < width)[:, None] & used[None, :]
    both = np.concatenate([np.where(live, np.cos(angle), 0.0), np.where(live, np.sin(angle), 0.0)], axis=1)
    high = both.astype(np.float32).astype(ml_dtypes.bfloat16)
    low = (both - high.astype(np.float64)).astype(np.float32).astype(ml_dtypes.bfloat16)
    residue = np.arange(8)
    twist = 2.0 * np.pi * ((residue[:, None] * position[None, :]) % (width * PARTS)) / (width * PARTS)
    twists = np.stack([np.cos(twist), np.sin(twist)]).astype(np.float32)
    return np.stack([high, low]), twists


def split(value):
    high = value.astype(jnp.bfloat16)
    return high, (value - high.astype(jnp.float32)).astype(jnp.bfloat16)


def wave_product(stack_ref, table_ref):
    rows = stack_ref.shape[0]
    high, low = split(stack_ref[...])
    lead = jnp.dot(jnp.concatenate([high, low], axis=0), table_ref[0], preferred_element_type=jnp.float32)
    rest = jnp.dot(high, table_ref[1], preferred_element_type=jnp.float32)
    return lead[:rows] + lead[rows:] + rest


def filter_blocks(blocks, result, stack, table, twists, cuts, width):
    rows, lanes = blocks.shape[1:]
    x = [blocks[d] for d in range(PARTS)]
    a = [x[d] + x[d + 4] for d in range(4)]
    b = [x[d] - x[d + 4] for d in range(4)]
    b_minus = (b[1] - b[3]) * ROOT_HALF
    b_plus = (b[1] + b[3]) * ROOT_HALF
    even, odd = a[0] + a[2], a[1] + a[3]
    waves = [
        (even + odd, None),
        (b[0] + b_minus, -b[2] - b_plus),
        (a[0] - a[2], a[3] - a[1]),
        (b[0] - b_minus, b[2] - b_plus),
        (even - odd, None),
    ]
    for r, (re, im) in enumerate(waves):
        if r == 0:
            new_re, new_im = re, jnp.zeros_like(re)
        else:
            c, s = twists[0, r : r + 1, :], twists[1, r : r + 1, :]
            new_re = re * c if im is None else re * c + im * s
            new_im = -re * s if im is None else im * c - re * s
        stack[8 * r : 8 * r + rows, :] = new_re
        stack[40 + 8 * r : 40 + 8 * r + rows, :] = new_im
    first = wave_product(stack, table)
    q = lax.broadcasted_iota(jnp.int32, (8, lanes), 1)
    row = lax.broadcasted_iota(jnp.int32, (8, lanes), 0)
    cut = jnp.where(lax.rem(row, 2) == 0, cuts[0], cuts[1])
    for r in range(5):
        wave = PARTS * q + r
        wave = jnp.minimum(wave, PARTS * width - wave).astype(jnp.float32)
        ratio = cut / jnp.maximum(wave, 1.0)
        weight = (1.0 if r in (0, 4) else 2.0) / (PARTS * width)
        factor = jnp.where(wave <= cut, 1.0, ratio * ratio) * weight
        factor = jnp.where(q < width, factor, 0.0)
        lo, hi = 8 * r, 40 + 8 * r
        re = first[lo : lo + 8, :lanes] + first[hi : hi + 8, lanes:]
        im = first[hi : hi + 8, :lanes] - first[lo : lo + 8, lanes:]
        stack[lo : lo + 8, :] = re * factor
        stack[hi : hi + 8, :] = im * factor
    second = wave_product(stack, table)
    back = []
    for r in range(5):
        lo, hi = 8 * r, 40 + 8 * r
        re = second[lo : lo + 8, :lanes] - second[hi : hi + 8, lanes:]
        if r == 0:
            back.append((re, None))
            continue
        im = second[hi : hi + 8, :lanes] + second[lo : lo + 8, lanes:]
        c, s = twists[0, r : r + 1, :], twists[1, r : r + 1, :]
        back.append((re * c - im * s, None if r == 4 else im * c + re * s))
    r0, r4 = back[0][0], back[4][0]
    (r1, i1), (r2, i2), (r3, i3) = back[1], back[2], back[3]
    plus, minus = r0 + r4, r0 - r4
    even_a, even_b = plus + r2, plus - r2
    odd_a, odd_b = minus - i2, minus + i2
    half = [
        r1 + r3,
        ((r1 - r3) - (i1 + i3)) * ROOT_HALF,
        i3 - i1,
        ((r3 - r1) - (i1 + i3)) * ROOT_HALF,
    ]
    base = [even_a, odd_a, even_b, odd_b]
    for d in range(4):
        result[d] = (base[d] + half[d])[:rows]
        result[d + 4] = (base[d] - half[d])[:rows]


def kernel(sizes, u_hbm, v_hbm, t_hbm, p_hbm, g_hbm, cut_ref, table_hbm, twists_hbm, packed,
           u_ref, v_ref, t_ref, p_ref, g_ref, twists, table, raw, pack, circles, stack, filtered, home, smooth,
           edge_out, edge_in, row_out, row_in, pole_in, ghost_out, ghost, ext, height, heights,
           input_sem, table_sem, edge_send, edge_recv, row_send, row_recv, pole_recv, circ_send, circ_recv,
           home_send, home_recv, ghost_send, ghost_recv, lev_send, lev_recv):
    lats, lons, levs, polar_ranks = sizes
    rows, width = p_ref.shape
    lanes = raw.shape[-1]
    lat, lon, lev = lax.axis_index("lat"), lax.axis_index("lon"), lax.axis_index("lev")
    polar_lat = lambda r: (r < polar_ranks) | (r >= lats - polar_ranks)
    polar = polar_lat(lat)
    far = lax.rem(lev + levs // 2, levs)
    south_filtered = (lat == 0) | polar_lat(lat - 1)
    north_filtered = (lat == lats - 1) | polar_lat(lat + 1)

    barrier = pltpu.get_barrier_semaphore()

    def greet(**where):
        pl.semaphore_signal(barrier, inc=1, device_id=where, device_id_type=MESH)

    for k in range(PARTS):
        greet(lon=lax.rem(lon + k, PARTS), lev=far)
    greet(lon=lax.rem(lon + 1, PARTS))
    greet(lon=lax.rem(lon + PARTS - 1, PARTS))
    for k in range(1, levs):
        if k != levs // 2:
            greet(lev=lax.rem(lev + k, levs))

    @pl.when(lat > 0)
    def _():
        greet(lat=lat - 1)

        @pl.when(south_filtered)
        def _():
            greet(lat=lat - 1, lon=PARTS - 1, lev=far)

    @pl.when(lat < lats - 1)
    def _():
        greet(lat=lat + 1)

        @pl.when(north_filtered)
        def _():
            greet(lat=lat + 1, lon=0, lev=far)

    input_copies = [
        pltpu.make_async_copy(src, dst, input_sem.at[k])
        for k, (src, dst) in enumerate(
            ((u_hbm, u_ref), (v_hbm, v_ref), (t_hbm, t_ref), (g_hbm, g_ref), (p_hbm, p_ref)))
    ]
    table_copies = [
        pltpu.make_async_copy(twists_hbm, twists, table_sem.at[0]),
        pltpu.make_async_copy(table_hbm, table, table_sem.at[1]),
    ]
    for copy in input_copies:
        copy.start()

    @pl.when(polar)
    def _():
        for copy in table_copies:
            copy.start()

    lane = lax.broadcasted_iota(jnp.int32, (rows, lanes), 1)
    last_tile = (width // 128) * 128
    for f, ref in enumerate((u_ref, v_ref, t_ref, g_ref, p_ref)):
        input_copies[f].wait()
        raw[f, :, last_tile:] = jnp.zeros((rows, lanes - last_tile), jnp.float32)
        raw[f, :, :width] = ref[...] if f == 4 else ref[0]
    raw_u, raw_v, raw_t, raw_g, raw_p = (raw[f] for f in range(5))
    small = lax.broadcasted_iota(jnp.int32, (rows, 128), 1)
    for side, column in ((0, 0), (1, width - 1)):
        edge = jnp.zeros((rows, 128), jnp.float32)
        for f, value in enumerate((raw_u, raw_t, raw_g, raw_p)):
            edge = jnp.where(small == f, value[:, column : column + 1], edge)
        edge_out[side] = edge
    for side, row in ((0, 0), (1, rows - 1)):
        for f, value in enumerate((raw_v, raw_t, raw_p)):
            row_out[side, f : f + 1, :] = value[row : row + 1]

    @pl.when(polar)
    def _():
        for e in range(PARTS):
            for f, value in enumerate((raw_u, raw_v, raw_t)):
                pack[e, 2 * f : 2 * f + 2, :] = value[2 * e : 2 * e + 2]

    count = lambda condition: jnp.where(condition, 1, 0)
    below, above = lat > 0, lat < lats - 1
    arrivals = PARTS + 2 + levs - 2 + count(below) + count(above)
    arrivals += PARTS * count(polar & ((below & (lon == 0)) | (above & (lon == PARTS - 1))))
    pl.semaphore_wait(barrier, arrivals)

    def send(src, dst, send_sem, recv_sem, **where):
        return pltpu.make_async_remote_copy(
            src_ref=src, dst_ref=dst, send_sem=send_sem, recv_sem=recv_sem,
            device_id=where, device_id_type=MESH)

    order = (4, 5, 3, 6, 2, 7, 1, 0)
    circ_copies = [
        send(pack.at[lax.rem(lon + k, PARTS)], circles.at[lon], circ_send.at[k], circ_recv.at[k],
             lon=lax.rem(lon + k, PARTS), lev=far)
        for k in order
    ]

    @pl.when(polar)
    def _():
        for copy in circ_copies:
            copy.start()

    edge_copies = [
        send(edge_out.at[0], edge_in.at[0], edge_send.at[0], edge_recv.at[0], lon=lax.rem(lon + PARTS - 1, PARTS)),
        send(edge_out.at[1], edge_in.at[1], edge_send.at[1], edge_recv.at[1], lon=lax.rem(lon + 1, PARTS)),
    ]
    for copy in edge_copies:
        copy.start()

    @pl.when(lat > 0)
    def _():
        send(row_out.at[0], row_in.at[1], row_send.at[0], row_recv.at[1], lat=lat - 1).start()

    @pl.when(lat == 0)
    def _():
        send(row_out.at[0], pole_in.at[lon], row_send.at[0], pole_recv.at[lon], lon=0, lev=far).start()

    @pl.when(lat < lats - 1)
    def _():
        send(row_out.at[1], row_in.at[0], row_send.at[1], row_recv.at[0], lat=lat + 1).start()

    @pl.when(lat == lats - 1)
    def _():
        send(row_out.at[1], pole_in.at[lon], row_send.at[1], pole_recv.at[lon], lon=PARTS - 1, lev=far).start()

    @pl.when(polar)
    def _():
        own = jnp.where(lat < polar_ranks, 0, 1)
        row = lat * rows + 2 * lon
        cuts = []
        for j in range(2):
            rank = jnp.where(own == 0, row + j, lats * rows - 1 - (row + j))
            cuts.append(cut_ref[own, rank].astype(jnp.float32))
        for copy in table_copies:
            copy.wait()
        for copy in circ_copies:
            copy.wait_recv()
        filter_blocks(circles, filtered, stack, table, twists, cuts, width)

    home_copies = [
        send(filtered.at[lax.rem(lon + k, PARTS)], home.at[lon], home_send.at[k], home_recv.at[k],
             lon=lax.rem(lon + k, PARTS), lev=far)
        for k in order
    ]

    def ghost_copy(d, side, **where):
        return send(ghost_out.at[d], ghost.at[side], ghost_send.at[d], ghost_recv.at[side], **where)

    def ghost_copies(act):
        @pl.when(polar & (lon == 0))
        def _():
            for d in range(PARTS):
                @pl.when(lat > 0)
                def _():
                    act(ghost_copy(d, 1, lat=lat - 1, lon=d, lev=far))

                @pl.when(lat == 0)
                def _():
                    act(ghost_copy(d, 0, lon=(d + PARTS // 2) % PARTS, lev=far))

        @pl.when(polar & (lon == PARTS - 1))
        def _():
            for d in range(PARTS):
                @pl.when(lat < lats - 1)
                def _():
                    act(ghost_copy(d, 0, lat=lat + 1, lon=d, lev=far))

                @pl.when(lat == lats - 1)
                def _():
                    act(ghost_copy(d, 1, lon=(d + PARTS // 2) % PARTS, lev=far))

    for edge_owner, row, at_pole in ((0, 0, lat == 0), (PARTS - 1, 1, lat == lats - 1)):
        @pl.when(polar & (lon == edge_owner))
        def _():
            for d in range(PARTS):
                ghost_out[d, 0:1, :] = filtered[d, 2 + row : 3 + row, :]
                ghost_out[d, 1:2, :] = filtered[d, 4 + row : 5 + row, :]
                ghost_out[d, 2:3, :] = jnp.zeros((1, lanes), jnp.float32)

            @pl.when(at_pole)
            def _():
                for d in range(PARTS):
                    pltpu.make_async_copy(row_out.at[row], pole_in.at[d], pole_recv.at[d]).wait()
                for d in range(PARTS):
                    ghost_out[d, 2:3, :] = pole_in[d, 2:3, :]

    @pl.when(polar)
    def _():
        for copy in home_copies:
            copy.start()

    ghost_copies(lambda copy: copy.start())

    for copy in edge_copies:
        copy.wait_recv()
    for side, present in ((0, lat > 0), (1, lat < lats - 1)):
        @pl.when(present)
        def _():
            pltpu.make_async_copy(row_out.at[side], row_in.at[side], row_recv.at[side]).wait()

    def with_edges(value, f):
        east, west = edge_in[0][:, f : f + 1], edge_in[1][:, f : f + 1]
        return jnp.where(lane == width, east, jnp.where(lane == lanes - 1, west, value))

    flow, pres = with_edges(raw_g, 2), with_edges(raw_p, 3)

    @pl.when(jnp.logical_not(polar))
    def _():
        smooth[0] = with_edges(raw_u, 0)
        smooth[1] = raw_v
        smooth[2] = with_edges(raw_t, 1)

    latitude = (lat * rows + lax.broadcasted_iota(jnp.int32, (rows, 128), 0)).astype(jnp.float32)
    latitude = ((latitude + 0.5) / (lats * rows) - 0.5) * jnp.float32(math.pi)
    scale = (zonal_courant / jnp.cos(latitude))[:, :1]
    coriolis = (coriolis_scale * jnp.sin(latitude))[:, :1]

    @pl.when(polar)
    def _():
        for copy in home_copies:
            copy.wait_recv()
        for e in range(PARTS):
            for f in range(3):
                smooth[f, 2 * e : 2 * e + 2, :] = home[e, 2 * f : 2 * f + 2, :]

    @pl.when(south_filtered)
    def _():
        pltpu.make_async_copy(ghost_out.at[0], ghost.at[0], ghost_recv.at[0]).wait()

    @pl.when(north_filtered)
    def _():
        pltpu.make_async_copy(ghost_out.at[0], ghost.at[1], ghost_recv.at[1]).wait()

    def zonal(value):
        return pltpu.roll(value, lanes - 1, 1) - pltpu.roll(value, 1, 1)

    fu, fv, ft = smooth[0], smooth[1], smooth[2]
    div = -heat_link_multiplier * ft - pres * (1.0 / levs)
    ext[0, 8 : 8 + rows, :] = fv
    ext[1, 8 : 8 + rows, :] = div
    for side, at in ((0, 7), (1, 8 + rows)):
        wanted = south_filtered if side == 0 else north_filtered
        pole = (lat == 0) if side == 0 else (lat == lats - 1)
        gv = jnp.where(wanted, ghost[side, 0:1, :], row_in[side, 0:1, :])
        gt = jnp.where(wanted, ghost[side, 1:2, :], row_in[side, 1:2, :])
        gp = jnp.where(pole, ghost[side, 2:3, :], row_in[side, 2:3, :])
        ext[0, at : at + 1, :] = jnp.where(pole, -gv, gv)
        ext[1, at : at + 1, :] = -heat_link_multiplier * gt - gp * (1.0 / levs)
    merid_v = ext[0, 9 : 9 + rows, :] - ext[0, 7 : 7 + rows, :]
    merid_div = ext[1, 9 : 9 + rows, :] - ext[1, 7 : 7 + rows, :]
    bar = scale * zonal(fu) + merid_courant * merid_v
    height[...] = bar
    lev_copies = [
        send(height, heights.at[k], lev_send.at[k], lev_recv.at[k], lev=lax.rem(lev + k, levs))
        for k in range(1, levs)
    ]
    for copy in lev_copies:
        copy.start()
    packed[0] = (raw_u - coriolis * fv - scale * zonal(div))
    packed[1] = (raw_v + coriolis * fu - merid_courant * merid_div)
    packed[2] = (raw_t + bar + scale * zonal(flow * ft))

    for copy in edge_copies:
        copy.wait_send()
    for side in range(2):
        pltpu.make_async_copy(row_out.at[side], row_in.at[side], row_send.at[side]).wait()

    @pl.when(polar)
    def _():
        for copy in circ_copies:
            copy.wait_send()
        for copy in home_copies:
            copy.wait_send()

    ghost_copies(lambda copy: copy.wait_send())
    total = raw_p + bar
    for copy in lev_copies:
        copy.wait_recv()
    for k in range(1, levs):
        total = total + heights[k]
    packed[3] = total
    for copy in lev_copies:
        copy.wait_send()


def unpack(packed, out_u, out_v, out_t, out_p):
    width = out_p.shape[-1]
    out_u[0] = packed[0, :, :width]
    out_v[0] = packed[1, :, :width]
    out_t[0] = packed[2, :, :width]
    out_p[...] = packed[3, :, :width]


def solution(mesh):
    lats, lons, levs = mesh.shape["lat"], mesh.shape["lon"], mesh.shape["lev"]
    field, plane = P("lev", "lat", "lon"), P("lat", "lon")

    def local(adjoint_u, adjoint_v, adjoint_temp, adjoint_pres, carrying_eastward_flow, cutoff):
        rows, width = adjoint_pres.shape
        lanes = (width + 2 + 127) // 128 * 128
        table, twists = wave_tables(width, lanes)
        sizes = (lats, lons, levs, cutoff.shape[1] // rows)
        vmem = pl.BlockSpec(memory_space=pltpu.VMEM)
        anywhere = pl.BlockSpec(memory_space=pl.ANY)
        f32, dma = jnp.float32, pltpu.SemaphoreType.DMA
        block = (PARTS, 6, lanes)
        packed = pl.pallas_call(
            functools.partial(kernel, sizes),
            name="adjoint_step",
            out_shape=jax.ShapeDtypeStruct((4, rows, lanes), f32),
            in_specs=[anywhere] * 5 + [pl.BlockSpec(memory_space=pltpu.SMEM)] + [anywhere] * 2,
            out_specs=vmem,
            scratch_shapes=[
                pltpu.VMEM((1, rows, width), f32),
                pltpu.VMEM((1, rows, width), f32),
                pltpu.VMEM((1, rows, width), f32),
                pltpu.VMEM((rows, width), f32),
                pltpu.VMEM((1, rows, width), f32),
                pltpu.VMEM(twists.shape, f32),
                pltpu.VMEM(table.shape, jnp.bfloat16),
                pltpu.VMEM((5, rows, lanes), f32),
                pltpu.VMEM(block, f32),
                pltpu.VMEM(block, f32),
                pltpu.VMEM((80, lanes), f32),
                pltpu.VMEM(block, f32),
                pltpu.VMEM(block, f32),
                pltpu.VMEM((3, rows, lanes), f32),
                pltpu.VMEM((2, rows, 128), f32),
                pltpu.VMEM((2, rows, 128), f32),
                pltpu.VMEM((2, 3, lanes), f32),
                pltpu.VMEM((2, 3, lanes), f32),
                pltpu.VMEM((PARTS, 3, lanes), f32),
                pltpu.VMEM((PARTS, 3, lanes), f32),
                pltpu.VMEM((2, 3, lanes), f32),
                pltpu.VMEM((2, rows + 16, lanes), f32),
                pltpu.VMEM((rows, lanes), f32),
                pltpu.VMEM((levs, rows, lanes), f32),
                dma((5,)), dma((2,)), dma((2,)), dma((2,)), dma((2,)), dma((2,)), dma((PARTS,)),
                dma((PARTS,)), dma((PARTS,)), dma((PARTS,)), dma((PARTS,)),
                dma((PARTS,)), dma((2,)), dma((levs,)), dma((levs,)),
            ],
            compiler_params=pltpu.CompilerParams(collective_id=0, has_side_effects=True),
        )(adjoint_u, adjoint_v, adjoint_temp, adjoint_pres, carrying_eastward_flow, cutoff,
          jnp.asarray(table), jnp.asarray(twists))
        return pl.pallas_call(
            unpack,
            name="hand_on",
            out_shape=[jax.ShapeDtypeStruct(adjoint_u.shape, f32)] * 3
            + [jax.ShapeDtypeStruct(adjoint_pres.shape, f32)],
            in_specs=[vmem],
            out_specs=[vmem] * 4,
        )(packed)

    return jax.shard_map(
        local, mesh=mesh, in_specs=(field, field, field, plane, field, P()),
        out_specs=(field, field, field, plane), check_vma=False)
```

```python
import functools
import math

import jax
import jax.numpy as jnp
import ml_dtypes
import numpy as np
from jax import lax
from jax.experimental import pallas as pl
from jax.experimental.pallas import tpu as pltpu
from jax.sharding import PartitionSpec as P

zonal_courant = 0.15
merid_courant = 0.15
coriolis_scale = 0.4
heat_link_multiplier = 0.3

MESH = pl.DeviceIdType.MESH
PARTS = 8
ROOT_HALF = math.sqrt(0.5)


def lane_positions(width, padded):
    position = np.zeros(padded, np.int64)
    position[:width] = np.arange(width)
    position[width] = width
    position[padded - 1] = -1
    used = np.zeros(padded, bool)
    used[: width + 1] = True
    used[padded - 1] = True
    return position, used


def wave_tables(width, padded):
    position, used = lane_positions(width, padded)
    index = np.arange(padded)
    angle = 2.0 * np.pi * ((index[:, None] * position[None, :]) % width) / width
    live = (index < width)[:, None] & used[None, :]
    both = np.concatenate([np.where(live, np.cos(angle), 0.0), np.where(live, np.sin(angle), 0.0)], axis=1)
    high = both.astype(np.float32).astype(ml_dtypes.bfloat16)
    low = (both - high.astype(np.float64)).astype(np.float32).astype(ml_dtypes.bfloat16)
    residue = np.arange(16) // 2
    twist = 2.0 * np.pi * ((residue[:, None] * position[None, :]) % (width * PARTS)) / (width * PARTS)
    twists = np.stack([np.cos(twist), np.sin(twist)]).astype(np.float32)
    return np.stack([high, low]), twists


def split(value):
    high = value.astype(jnp.bfloat16)
    return high, (value - high.astype(jnp.float32)).astype(jnp.bfloat16)


def wave_product(stack_ref, table_ref):
    rows = stack_ref.shape[0]
    high, low = split(stack_ref[...])
    lead = jnp.dot(jnp.concatenate([high, low], axis=0), table_ref[0], preferred_element_type=jnp.float32)
    rest = jnp.dot(high, table_ref[1], preferred_element_type=jnp.float32)
    return lead[:rows] + lead[rows:] + rest


def damping(cuts, lanes, width):
    q = lax.broadcasted_iota(jnp.int32, (16, lanes), 1)
    row = lax.broadcasted_iota(jnp.int32, (16, lanes), 0)
    residue = lax.shift_right_logical(row, 1)
    cut = jnp.where(row == 2 * residue, cuts[0], cuts[1])
    wave = PARTS * q + residue
    wave = jnp.minimum(wave, PARTS * width - wave).astype(jnp.float32)
    ratio = cut / jnp.maximum(wave, 1.0)
    weight = jnp.where((residue == 0) | (residue == 4), 1.0, 2.0) * (1.0 / (PARTS * width))
    factor = jnp.where(wave <= cut, 1.0, ratio * ratio) * weight
    return jnp.where(q < width, factor, 0.0)


def filter_blocks(blocks, result, stack, table, twists, factor):
    lanes = blocks.shape[-1]
    x = [blocks[d] for d in range(PARTS)]
    a = [x[d] + x[d + 4] for d in range(4)]
    b = [x[d] - x[d + 4] for d in range(4)]
    b_minus = (b[1] - b[3]) * ROOT_HALF
    b_plus = (b[1] + b[3]) * ROOT_HALF
    even, odd = a[0] + a[2], a[1] + a[3]
    waves = [
        (even + odd, None),
        (b[0] + b_minus, -b[2] - b_plus),
        (a[0] - a[2], a[3] - a[1]),
        (b[0] - b_minus, b[2] - b_plus),
        (even - odd, None),
    ]
    for r, (re, im) in enumerate(waves):
        stack[2 * r : 2 * r + 2, :] = re
        stack[16 + 2 * r : 18 + 2 * r, :] = jnp.zeros_like(re) if im is None else im
    c, s = twists[0], twists[1]
    re, im = stack[:16], stack[16:]
    stack[:16] = re * c + im * s
    stack[16:] = im * c - re * s
    first = wave_product(stack, table)
    stack[:16] = (first[:16, :lanes] + first[16:, lanes:]) * factor
    stack[16:] = (first[16:, :lanes] - first[:16, lanes:]) * factor
    second = wave_product(stack, table)
    re = second[:16, :lanes] - second[16:, lanes:]
    im = second[16:, :lanes] + second[:16, lanes:]
    back_re, back_im = re * c - im * s, im * c + re * s
    r0, r1, r2, r3, r4 = (back_re[2 * r : 2 * r + 2] for r in range(5))
    i1, i2, i3 = (back_im[2 * r : 2 * r + 2] for r in range(1, 4))
    plus, minus = r0 + r4, r0 - r4
    base = [plus + r2, minus - i2, plus - r2, minus + i2]
    half = [
        r1 + r3,
        ((r1 - r3) - (i1 + i3)) * ROOT_HALF,
        i3 - i1,
        ((r3 - r1) - (i1 + i3)) * ROOT_HALF,
    ]
    for d in range(4):
        result[d] = base[d] + half[d]
        result[d + 4] = base[d] - half[d]


def kernel(sizes, u_hbm, v_hbm, t_hbm, p_hbm, g_hbm, cut_ref, table_hbm, twists_hbm, packed,
           u_ref, v_ref, t_ref, p_ref, g_ref, twists, table, raw, pack, circles, stack, filtered, home, smooth,
           edge_out, edge_in, row_out, row_in, pole_in, ghost_v_out, ghost_t_out, ghost_v, ghost_t, ext, height, heights,
           input_sem, table_sem, edge_send, edge_recv, row_send, row_recv, pole_recv, circ_send, circ_recv,
           home_send, home_recv, ghost_send, ghost_recv, lev_send, lev_recv):
    lats, lons, levs, polar_ranks = sizes
    rows, width = p_ref.shape
    lanes = raw.shape[-1]
    lat, lon, lev = lax.axis_index("lat"), lax.axis_index("lon"), lax.axis_index("lev")
    polar_lat = lambda r: (r < polar_ranks) | (r >= lats - polar_ranks)
    polar = polar_lat(lat)
    far = lax.rem(lev + levs // 2, levs)
    south_filtered = (lat == 0) | polar_lat(lat - 1)
    north_filtered = (lat == lats - 1) | polar_lat(lat + 1)

    barrier = pltpu.get_barrier_semaphore()

    def greet(**where):
        pl.semaphore_signal(barrier, inc=1, device_id=where, device_id_type=MESH)

    for k in range(PARTS):
        greet(lon=lax.rem(lon + k, PARTS), lev=far)
    greet(lon=lax.rem(lon + 1, PARTS))
    greet(lon=lax.rem(lon + PARTS - 1, PARTS))
    for k in range(1, levs):
        if k != levs // 2:
            greet(lev=lax.rem(lev + k, levs))

    @pl.when(lat > 0)
    def _():
        greet(lat=lat - 1)

        @pl.when(south_filtered)
        def _():
            greet(lat=lat - 1, lon=PARTS - 1, lev=far)

    @pl.when(lat < lats - 1)
    def _():
        greet(lat=lat + 1)

        @pl.when(north_filtered)
        def _():
            greet(lat=lat + 1, lon=0, lev=far)

    input_copies = [
        pltpu.make_async_copy(src, dst, input_sem.at[k])
        for k, (src, dst) in enumerate(
            ((u_hbm, u_ref), (v_hbm, v_ref), (t_hbm, t_ref), (g_hbm, g_ref), (p_hbm, p_ref)))
    ]
    table_copies = [
        pltpu.make_async_copy(twists_hbm, twists, table_sem.at[0]),
        pltpu.make_async_copy(table_hbm, table, table_sem.at[1]),
    ]
    for copy in input_copies:
        copy.start()

    @pl.when(polar)
    def _():
        for copy in table_copies:
            copy.start()

    lane = lax.broadcasted_iota(jnp.int32, (rows, lanes), 1)
    last_tile = (width // 128) * 128
    for f, ref in enumerate((u_ref, v_ref, t_ref, g_ref, p_ref)):
        input_copies[f].wait()
        raw[f, :, last_tile:] = jnp.zeros((rows, lanes - last_tile), jnp.float32)
        raw[f, :, :width] = ref[...] if f == 4 else ref[0]
    raw_u, raw_v, raw_t, raw_g, raw_p = (raw[f] for f in range(5))
    small = lax.broadcasted_iota(jnp.int32, (rows, 128), 1)
    for side, column in ((0, 0), (1, width - 1)):
        edge = jnp.zeros((rows, 128), jnp.float32)
        for f, value in enumerate((raw_u, raw_t, raw_g, raw_p)):
            edge = jnp.where(small == f, value[:, column : column + 1], edge)
        edge_out[side] = edge
    for side, row in ((0, 0), (1, rows - 1)):
        for f, value in enumerate((raw_v, raw_t, raw_p)):
            row_out[side, f : f + 1, :] = value[row : row + 1]

    @pl.when(polar)
    def _():
        stack[...] = jnp.zeros_like(stack)
        for f, value in enumerate((raw_u, raw_v, raw_t)):
            for e in range(PARTS):
                pack[f, e] = value[2 * e : 2 * e + 2]

    latitude = (lat * rows + lax.broadcasted_iota(jnp.int32, (rows, 128), 0)).astype(jnp.float32)
    latitude = ((latitude + 0.5) / (lats * rows) - 0.5) * jnp.float32(math.pi)
    scale = (zonal_courant / jnp.cos(latitude))[:, :1]
    coriolis = (coriolis_scale * jnp.sin(latitude))[:, :1]

    count = lambda condition: jnp.where(condition, 1, 0)
    below, above = lat > 0, lat < lats - 1
    arrivals = PARTS + 2 + levs - 2 + count(below) + count(above)
    arrivals += PARTS * count(polar & ((below & (lon == 0)) | (above & (lon == PARTS - 1))))
    pl.semaphore_wait(barrier, arrivals)

    def send(src, dst, send_sem, recv_sem, **where):
        return pltpu.make_async_remote_copy(
            src_ref=src, dst_ref=dst, send_sem=send_sem, recv_sem=recv_sem,
            device_id=where, device_id_type=MESH)

    order = (4, 5, 3, 6, 2, 7, 1, 0)
    circ_copies = [
        [send(pack.at[f, lax.rem(lon + k, PARTS)], circles.at[f, lon], circ_send.at[f, k], circ_recv.at[f, k],
              lon=lax.rem(lon + k, PARTS), lev=far)
         for k in order]
        for f in range(3)
    ]

    @pl.when(polar)
    def _():
        for copies in circ_copies:
            for copy in copies:
                copy.start()

    edge_copies = [
        send(edge_out.at[0], edge_in.at[0], edge_send.at[0], edge_recv.at[0], lon=lax.rem(lon + PARTS - 1, PARTS)),
        send(edge_out.at[1], edge_in.at[1], edge_send.at[1], edge_recv.at[1], lon=lax.rem(lon + 1, PARTS)),
    ]
    for copy in edge_copies:
        copy.start()

    @pl.when(lat > 0)
    def _():
        send(row_out.at[0], row_in.at[1], row_send.at[0], row_recv.at[1], lat=lat - 1).start()

    @pl.when(lat == 0)
    def _():
        send(row_out.at[0], pole_in.at[lon], row_send.at[0], pole_recv.at[lon], lon=0, lev=far).start()

    @pl.when(lat < lats - 1)
    def _():
        send(row_out.at[1], row_in.at[0], row_send.at[1], row_recv.at[0], lat=lat + 1).start()

    @pl.when(lat == lats - 1)
    def _():
        send(row_out.at[1], pole_in.at[lon], row_send.at[1], pole_recv.at[lon], lon=PARTS - 1, lev=far).start()

    home_copies = [
        [send(filtered.at[f, lax.rem(lon + k, PARTS)], home.at[f, lon], home_send.at[f, k], home_recv.at[f, k],
              lon=lax.rem(lon + k, PARTS), lev=far)
         for k in order]
        for f in range(3)
    ]

    def ghost_copies(g, act):
        out, into = ((ghost_v_out, ghost_v), (ghost_t_out, ghost_t))[g]

        def copy(d, side, **where):
            return send(out.at[d], into.at[side], ghost_send.at[g, d], ghost_recv.at[g, side], **where)

        @pl.when(polar & (lon == 0))
        def _():
            for d in range(PARTS):
                @pl.when(lat > 0)
                def _():
                    act(copy(d, 1, lat=lat - 1, lon=d, lev=far))

                @pl.when(lat == 0)
                def _():
                    act(copy(d, 0, lon=(d + PARTS // 2) % PARTS, lev=far))

        @pl.when(polar & (lon == PARTS - 1))
        def _():
            for d in range(PARTS):
                @pl.when(lat < lats - 1)
                def _():
                    act(copy(d, 0, lat=lat + 1, lon=d, lev=far))

                @pl.when(lat == lats - 1)
                def _():
                    act(copy(d, 1, lon=(d + PARTS // 2) % PARTS, lev=far))

    def start(copy):
        copy.start()

    @pl.when(polar)
    def _():
        own = jnp.where(lat < polar_ranks, 0, 1)
        first_row = lat * rows + 2 * lon
        cuts = []
        for j in range(2):
            rank = jnp.where(own == 0, first_row + j, lats * rows - 1 - (first_row + j))
            cuts.append(cut_ref[own, rank].astype(jnp.float32))
        factor = damping(cuts, lanes, width)
        for copy in table_copies:
            copy.wait()
        for f in range(3):
            for copy in circ_copies[f]:
                copy.wait_recv()
            filter_blocks(circles.at[f], filtered.at[f], stack, table, twists, factor)
            if f == 0:
                for copy in home_copies[f]:
                    copy.start()
                continue
            for edge_owner, row, at_pole in ((0, 0, lat == 0), (PARTS - 1, 1, lat == lats - 1)):
                @pl.when(lon == edge_owner)
                def _():
                    for d in range(PARTS):
                        if f == 1:
                            ghost_v_out[d] = filtered[f, d, row : row + 1, :]
                        else:
                            ghost_t_out[d, 0:1, :] = filtered[f, d, row : row + 1, :]
                    if f == 1:
                        for d in range(PARTS):
                            ghost_t_out[d, 1:2, :] = jnp.zeros((1, lanes), jnp.float32)

                        @pl.when(at_pole)
                        def _():
                            for d in range(PARTS):
                                pltpu.make_async_copy(row_out.at[row], pole_in.at[d], pole_recv.at[d]).wait()
                            for d in range(PARTS):
                                ghost_t_out[d, 1:2, :] = pole_in[d, 2:3, :]

            ghost_copies(f - 1, start)
            for copy in home_copies[f]:
                copy.start()

    for copy in edge_copies:
        copy.wait_recv()
    for side, present in ((0, lat > 0), (1, lat < lats - 1)):
        @pl.when(present)
        def _():
            pltpu.make_async_copy(row_out.at[side], row_in.at[side], row_recv.at[side]).wait()

    def with_edges(value, f):
        east, west = edge_in[0][:, f : f + 1], edge_in[1][:, f : f + 1]
        return jnp.where(lane == width, east, jnp.where(lane == lanes - 1, west, value))

    flow, pres = with_edges(raw_g, 2), with_edges(raw_p, 3)

    @pl.when(jnp.logical_not(polar))
    def _():
        smooth[0] = with_edges(raw_u, 0)
        smooth[1] = raw_v
        smooth[2] = with_edges(raw_t, 1)

    def gather(f):
        @pl.when(polar)
        def _():
            for copy in home_copies[f]:
                copy.wait_recv()
            for e in range(PARTS):
                smooth[f, 2 * e : 2 * e + 2, :] = home[f, e]

    poles = (lat == 0, lat == lats - 1)

    def ghosts(g):
        out, into = ((ghost_v_out, ghost_v), (ghost_t_out, ghost_t))[g]
        picked = []
        for side, wanted in ((0, south_filtered), (1, north_filtered)):
            @pl.when(wanted)
            def _():
                pltpu.make_async_copy(out.at[0], into.at[side], ghost_recv.at[g, side]).wait()

            picked.append(jnp.where(wanted, into[side, 0:1, :], row_in[side, g : g + 1, :]))
        return picked

    def merid(f, main, south, north):
        ext[f, 8 : 8 + rows, :] = main
        ext[f, 7:8, :] = south
        ext[f, 8 + rows : 9 + rows, :] = north
        return ext[f, 9 : 9 + rows, :] - ext[f, 7 : 7 + rows, :]

    def zonal(value):
        return pltpu.roll(value, lanes - 1, 1) - pltpu.roll(value, 1, 1)

    gather(0)
    gather(1)
    fu, fv = smooth[0], smooth[1]
    beyond = [jnp.where(poles[side], -g, g) for side, g in enumerate(ghosts(0))]
    bar = scale * zonal(fu) + merid_courant * merid(0, fv, *beyond)
    height[...] = bar
    lev_copies = [
        send(height, heights.at[k], lev_send.at[k], lev_recv.at[k], lev=lax.rem(lev + k, levs))
        for k in range(1, levs)
    ]
    for copy in lev_copies:
        copy.start()
    gather(2)
    ft = smooth[2]
    div = -heat_link_multiplier * ft - pres * (1.0 / levs)
    beyond = []
    for side, g in enumerate(ghosts(1)):
        gp = jnp.where(poles[side], ghost_t[side, 1:2, :], row_in[side, 2:3, :])
        beyond.append(-heat_link_multiplier * g - gp * (1.0 / levs))
    packed[0] = raw_u - coriolis * fv - scale * zonal(div)
    packed[1] = raw_v + coriolis * fu - merid_courant * merid(1, div, *beyond)
    packed[2] = raw_t + bar + scale * zonal(flow * ft)

    for copy in edge_copies:
        copy.wait_send()
    for side in range(2):
        pltpu.make_async_copy(row_out.at[side], row_in.at[side], row_send.at[side]).wait()

    @pl.when(polar)
    def _():
        for copies in circ_copies + home_copies:
            for copy in copies:
                copy.wait_send()

    for g in range(2):
        ghost_copies(g, lambda copy: copy.wait_send())
    total = raw_p + bar
    for copy in lev_copies:
        copy.wait_recv()
    for k in range(1, levs):
        total = total + heights[k]
    packed[3] = total
    for copy in lev_copies:
        copy.wait_send()


def unpack(packed, out_u, out_v, out_t, out_p):
    width = out_p.shape[-1]
    out_u[0] = packed[0, :, :width]
    out_v[0] = packed[1, :, :width]
    out_t[0] = packed[2, :, :width]
    out_p[...] = packed[3, :, :width]


def solution(mesh):
    lats, lons, levs = mesh.shape["lat"], mesh.shape["lon"], mesh.shape["lev"]
    field, plane = P("lev", "lat", "lon"), P("lat", "lon")

    def local(adjoint_u, adjoint_v, adjoint_temp, adjoint_pres, carrying_eastward_flow, cutoff):
        rows, width = adjoint_pres.shape
        lanes = (width + 2 + 127) // 128 * 128
        table, twists = wave_tables(width, lanes)
        sizes = (lats, lons, levs, cutoff.shape[1] // rows)
        vmem = pl.BlockSpec(memory_space=pltpu.VMEM)
        anywhere = pl.BlockSpec(memory_space=pl.ANY)
        f32, dma = jnp.float32, pltpu.SemaphoreType.DMA
        block = (3, PARTS, 2, lanes)
        packed = pl.pallas_call(
            functools.partial(kernel, sizes),
            name="adjoint_step",
            out_shape=jax.ShapeDtypeStruct((4, rows, lanes), f32),
            in_specs=[anywhere] * 5 + [pl.BlockSpec(memory_space=pltpu.SMEM)] + [anywhere] * 2,
            out_specs=vmem,
            scratch_shapes=[
                pltpu.VMEM((1, rows, width), f32),
                pltpu.VMEM((1, rows, width), f32),
                pltpu.VMEM((1, rows, width), f32),
                pltpu.VMEM((rows, width), f32),
                pltpu.VMEM((1, rows, width), f32),
                pltpu.VMEM(twists.shape, f32),
                pltpu.VMEM(table.shape, jnp.bfloat16),
                pltpu.VMEM((5, rows, lanes), f32),
                pltpu.VMEM(block, f32),
                pltpu.VMEM(block, f32),
                pltpu.VMEM((32, lanes), f32),
                pltpu.VMEM(block, f32),
                pltpu.VMEM(block, f32),
                pltpu.VMEM((3, rows, lanes), f32),
                pltpu.VMEM((2, rows, 128), f32),
                pltpu.VMEM((2, rows, 128), f32),
                pltpu.VMEM((2, 3, lanes), f32),
                pltpu.VMEM((2, 3, lanes), f32),
                pltpu.VMEM((PARTS, 3, lanes), f32),
                pltpu.VMEM((PARTS, 1, lanes), f32),
                pltpu.VMEM((PARTS, 2, lanes), f32),
                pltpu.VMEM((2, 1, lanes), f32),
                pltpu.VMEM((2, 2, lanes), f32),
                pltpu.VMEM((2, rows + 16, lanes), f32),
                pltpu.VMEM((rows, lanes), f32),
                pltpu.VMEM((levs, rows, lanes), f32),
                dma((5,)), dma((2,)), dma((2,)), dma((2,)), dma((2,)), dma((2,)), dma((PARTS,)),
                dma((3, PARTS)), dma((3, PARTS)), dma((3, PARTS)), dma((3, PARTS)),
                dma((2, PARTS)), dma((2, 2)), dma((levs,)), dma((levs,)),
            ],
            compiler_params=pltpu.CompilerParams(collective_id=0, has_side_effects=True),
        )(adjoint_u, adjoint_v, adjoint_temp, adjoint_pres, carrying_eastward_flow, cutoff,
          jnp.asarray(table), jnp.asarray(twists))
        return pl.pallas_call(
            unpack,
            name="hand_on",
            out_shape=[jax.ShapeDtypeStruct(adjoint_u.shape, f32)] * 3
            + [jax.ShapeDtypeStruct(adjoint_pres.shape, f32)],
            in_specs=[vmem],
            out_specs=[vmem] * 4,
        )(packed)

    return jax.shard_map(
        local, mesh=mesh, in_specs=(field, field, field, plane, field, P()),
        out_specs=(field, field, field, plane), check_vma=False)
```

```python
import functools
import math

import jax
import jax.numpy as jnp
import ml_dtypes
import numpy as np
from jax import lax
from jax.experimental import pallas as pl
from jax.experimental.pallas import tpu as pltpu
from jax.sharding import PartitionSpec as P

zonal_courant = 0.15
merid_courant = 0.15
coriolis_scale = 0.4
heat_link_multiplier = 0.3

MESH = pl.DeviceIdType.MESH
PARTS = 8
ROOT_HALF = math.sqrt(0.5)


def lane_positions(width, padded):
    position = np.zeros(padded, np.int64)
    position[:width] = np.arange(width)
    position[width] = width
    position[padded - 1] = -1
    used = np.zeros(padded, bool)
    used[: width + 1] = True
    used[padded - 1] = True
    return position, used


def wave_tables(width, padded):
    position, used = lane_positions(width, padded)
    index = np.arange(padded)
    angle = 2.0 * np.pi * ((index[:, None] * position[None, :]) % width) / width
    live = (index < width)[:, None] & used[None, :]
    both = np.concatenate([np.where(live, np.cos(angle), 0.0), np.where(live, np.sin(angle), 0.0)], axis=1)
    high = both.astype(np.float32).astype(ml_dtypes.bfloat16)
    low = (both - high.astype(np.float64)).astype(np.float32).astype(ml_dtypes.bfloat16)
    residue = np.arange(16) // 2
    twist = 2.0 * np.pi * ((residue[:, None] * position[None, :]) % (width * PARTS)) / (width * PARTS)
    twists = np.stack([np.cos(twist), np.sin(twist)]).astype(np.float32)
    return np.stack([high, low]), twists


def split(value):
    high = value.astype(jnp.bfloat16)
    return high, (value - high.astype(jnp.float32)).astype(jnp.bfloat16)


def wave_product(stack_ref, table_ref):
    rows = stack_ref.shape[0]
    high, low = split(stack_ref[...])
    lead = jnp.dot(jnp.concatenate([high, low], axis=0), table_ref[0], preferred_element_type=jnp.float32)
    rest = jnp.dot(high, table_ref[1], preferred_element_type=jnp.float32)
    return lead[:rows] + lead[rows:] + rest


def damping(cuts, lanes, width):
    q = lax.broadcasted_iota(jnp.int32, (16, lanes), 1)
    row = lax.broadcasted_iota(jnp.int32, (16, lanes), 0)
    residue = lax.shift_right_logical(row, 1)
    cut = jnp.where(row == 2 * residue, cuts[0], cuts[1])
    wave = PARTS * q + residue
    wave = jnp.minimum(wave, PARTS * width - wave).astype(jnp.float32)
    ratio = cut / jnp.maximum(wave, 1.0)
    weight = jnp.where((residue == 0) | (residue == 4), 1.0, 2.0) * (1.0 / (PARTS * width))
    factor = jnp.where(wave <= cut, 1.0, ratio * ratio) * weight
    return jnp.where(q < width, factor, 0.0)


def filter_blocks(blocks, result, stack, table, twists, factor):
    lanes = blocks.shape[-1]
    x = [blocks[d] for d in range(PARTS)]
    a = [x[d] + x[d + 4] for d in range(4)]
    b = [x[d] - x[d + 4] for d in range(4)]
    b_minus = (b[1] - b[3]) * ROOT_HALF
    b_plus = (b[1] + b[3]) * ROOT_HALF
    even, odd = a[0] + a[2], a[1] + a[3]
    waves = [
        (even + odd, None),
        (b[0] + b_minus, -b[2] - b_plus),
        (a[0] - a[2], a[3] - a[1]),
        (b[0] - b_minus, b[2] - b_plus),
        (even - odd, None),
    ]
    for r, (re, im) in enumerate(waves):
        stack[2 * r : 2 * r + 2, :] = re
        stack[16 + 2 * r : 18 + 2 * r, :] = jnp.zeros_like(re) if im is None else im
    c, s = twists[0], twists[1]
    re, im = stack[:16], stack[16:]
    stack[:16] = re * c + im * s
    stack[16:] = im * c - re * s
    first = wave_product(stack, table)
    stack[:16] = (first[:16, :lanes] + first[16:, lanes:]) * factor
    stack[16:] = (first[16:, :lanes] - first[:16, lanes:]) * factor
    second = wave_product(stack, table)
    re = second[:16, :lanes] - second[16:, lanes:]
    im = second[16:, :lanes] + second[:16, lanes:]
    back_re, back_im = re * c - im * s, im * c + re * s
    r0, r1, r2, r3, r4 = (back_re[2 * r : 2 * r + 2] for r in range(5))
    i1, i2, i3 = (back_im[2 * r : 2 * r + 2] for r in range(1, 4))
    plus, minus = r0 + r4, r0 - r4
    base = [plus + r2, minus - i2, plus - r2, minus + i2]
    half = [
        r1 + r3,
        ((r1 - r3) - (i1 + i3)) * ROOT_HALF,
        i3 - i1,
        ((r3 - r1) - (i1 + i3)) * ROOT_HALF,
    ]
    for d in range(4):
        result[d] = base[d] + half[d]
        result[d + 4] = base[d] - half[d]


def kernel(sizes, u_hbm, v_hbm, t_hbm, p_hbm, g_hbm, cut_hbm, table_hbm, twists_hbm, packed,
           u_ref, v_ref, t_ref, p_ref, g_ref, cut_ref, twists, table, raw, pack, circles, stack, filtered, home, smooth,
           edge_out, edge_in, row_out, row_in, pole_in, ghost_v_out, ghost_t_out, ghost_v, ghost_t, ext, height, heights,
           input_sem, table_sem, edge_send, edge_recv, row_send, row_recv, pole_recv, circ_send, circ_recv,
           home_send, home_recv, ghost_send, ghost_recv, lev_send, lev_recv):
    lats, lons, levs, polar_ranks = sizes
    rows, width = p_ref.shape
    lanes = raw.shape[-1]
    lat, lon, lev = lax.axis_index("lat"), lax.axis_index("lon"), lax.axis_index("lev")
    polar_lat = lambda r: (r < polar_ranks) | (r >= lats - polar_ranks)
    polar = polar_lat(lat)
    far = lax.rem(lev + levs // 2, levs)
    south_filtered = (lat == 0) | polar_lat(lat - 1)
    north_filtered = (lat == lats - 1) | polar_lat(lat + 1)

    barrier = pltpu.get_barrier_semaphore()

    def greet(**where):
        pl.semaphore_signal(barrier, inc=1, device_id=where, device_id_type=MESH)

    for k in range(PARTS):
        greet(lon=lax.rem(lon + k, PARTS), lev=far)
    greet(lon=lax.rem(lon + 1, PARTS))
    greet(lon=lax.rem(lon + PARTS - 1, PARTS))
    for k in range(1, levs):
        if k != levs // 2:
            greet(lev=lax.rem(lev + k, levs))

    @pl.when(lat > 0)
    def _():
        greet(lat=lat - 1)

        @pl.when(south_filtered)
        def _():
            greet(lat=lat - 1, lon=PARTS - 1, lev=far)

    @pl.when(lat < lats - 1)
    def _():
        greet(lat=lat + 1)

        @pl.when(north_filtered)
        def _():
            greet(lat=lat + 1, lon=0, lev=far)

    input_copies = [
        pltpu.make_async_copy(src, dst, input_sem.at[k])
        for k, (src, dst) in enumerate(
            ((u_hbm, u_ref), (v_hbm, v_ref), (t_hbm, t_ref), (g_hbm, g_ref), (p_hbm, p_ref)))
    ]
    table_copies = [
        pltpu.make_async_copy(twists_hbm, twists, table_sem.at[0]),
        pltpu.make_async_copy(table_hbm, table, table_sem.at[1]),
        pltpu.make_async_copy(cut_hbm, cut_ref, table_sem.at[2]),
    ]
    for copy in input_copies:
        copy.start()

    @pl.when(polar)
    def _():
        for copy in table_copies:
            copy.start()

    lane = lax.broadcasted_iota(jnp.int32, (rows, lanes), 1)
    last_tile = (width // 128) * 128
    for f, ref in enumerate((u_ref, v_ref, t_ref, g_ref, p_ref)):
        input_copies[f].wait()
        raw[f, :, last_tile:] = jnp.zeros((rows, lanes - last_tile), jnp.float32)
        raw[f, :, :width] = ref[...] if f == 4 else ref[0]
    raw_u, raw_v, raw_t, raw_g, raw_p = (raw[f] for f in range(5))
    small = lax.broadcasted_iota(jnp.int32, (rows, 128), 1)
    for side, column in ((0, 0), (1, width - 1)):
        edge = jnp.zeros((rows, 128), jnp.float32)
        for f, value in enumerate((raw_u, raw_t, raw_g, raw_p)):
            edge = jnp.where(small == f, value[:, column : column + 1], edge)
        edge_out[side] = edge
    for side, row in ((0, 0), (1, rows - 1)):
        for f, value in enumerate((raw_v, raw_t, raw_p)):
            row_out[side, f : f + 1, :] = value[row : row + 1]

    @pl.when(polar)
    def _():
        stack[...] = jnp.zeros_like(stack)
        for f, value in enumerate((raw_u, raw_v, raw_t)):
            for e in range(PARTS):
                pack[f, e] = value[2 * e : 2 * e + 2]

    latitude = (lat * rows + lax.broadcasted_iota(jnp.int32, (rows, 128), 0)).astype(jnp.float32)
    latitude = ((latitude + 0.5) / (lats * rows) - 0.5) * jnp.float32(math.pi)
    scale = (zonal_courant / jnp.cos(latitude))[:, :1]
    coriolis = (coriolis_scale * jnp.sin(latitude))[:, :1]

    count = lambda condition: jnp.where(condition, 1, 0)
    below, above = lat > 0, lat < lats - 1
    arrivals = PARTS + 2 + levs - 2 + count(below) + count(above)
    arrivals += PARTS * count(polar & ((below & (lon == 0)) | (above & (lon == PARTS - 1))))
    pl.semaphore_wait(barrier, arrivals)

    def send(src, dst, send_sem, recv_sem, **where):
        return pltpu.make_async_remote_copy(
            src_ref=src, dst_ref=dst, send_sem=send_sem, recv_sem=recv_sem,
            device_id=where, device_id_type=MESH)

    order = (4, 5, 3, 6, 2, 7, 1, 0)
    sequence = (1, 0, 2)
    circ_copies = [
        [send(pack.at[f, lax.rem(lon + k, PARTS)], circles.at[f, lon], circ_send.at[f, k], circ_recv.at[f, k],
              lon=lax.rem(lon + k, PARTS), lev=far)
         for k in order]
        for f in range(3)
    ]

    @pl.when(polar)
    def _():
        for f in sequence:
            for copy in circ_copies[f]:
                copy.start()

    edge_copies = [
        send(edge_out.at[0], edge_in.at[0], edge_send.at[0], edge_recv.at[0], lon=lax.rem(lon + PARTS - 1, PARTS)),
        send(edge_out.at[1], edge_in.at[1], edge_send.at[1], edge_recv.at[1], lon=lax.rem(lon + 1, PARTS)),
    ]
    for copy in edge_copies:
        copy.start()

    @pl.when(lat > 0)
    def _():
        send(row_out.at[0], row_in.at[1], row_send.at[0], row_recv.at[1], lat=lat - 1).start()

    @pl.when(lat == 0)
    def _():
        send(row_out.at[0], pole_in.at[lon], row_send.at[0], pole_recv.at[lon], lon=0, lev=far).start()

    @pl.when(lat < lats - 1)
    def _():
        send(row_out.at[1], row_in.at[0], row_send.at[1], row_recv.at[0], lat=lat + 1).start()

    @pl.when(lat == lats - 1)
    def _():
        send(row_out.at[1], pole_in.at[lon], row_send.at[1], pole_recv.at[lon], lon=PARTS - 1, lev=far).start()

    home_copies = [
        [send(filtered.at[f, lax.rem(lon + k, PARTS)], home.at[f, lon], home_send.at[f, k], home_recv.at[f, k],
              lon=lax.rem(lon + k, PARTS), lev=far)
         for k in order]
        for f in range(3)
    ]

    def ghost_copies(g, act):
        out, into = ((ghost_v_out, ghost_v), (ghost_t_out, ghost_t))[g]

        def copy(d, side, **where):
            return send(out.at[d], into.at[side], ghost_send.at[g, d], ghost_recv.at[g, side], **where)

        @pl.when(polar & (lon == 0))
        def _():
            for d in range(PARTS):
                @pl.when(lat > 0)
                def _():
                    act(copy(d, 1, lat=lat - 1, lon=d, lev=far))

                @pl.when(lat == 0)
                def _():
                    act(copy(d, 0, lon=(d + PARTS // 2) % PARTS, lev=far))

        @pl.when(polar & (lon == PARTS - 1))
        def _():
            for d in range(PARTS):
                @pl.when(lat < lats - 1)
                def _():
                    act(copy(d, 0, lat=lat + 1, lon=d, lev=far))

                @pl.when(lat == lats - 1)
                def _():
                    act(copy(d, 1, lon=(d + PARTS // 2) % PARTS, lev=far))

    def start(copy):
        copy.start()

    @pl.when(polar)
    def _():
        for copy in table_copies:
            copy.wait()
        own = jnp.where(lat < polar_ranks, 0, 1)
        first_row = lat * rows + 2 * lon
        cuts = []
        for j in range(2):
            rank = jnp.where(own == 0, first_row + j, lats * rows - 1 - (first_row + j))
            cuts.append(cut_ref[own, rank].astype(jnp.float32))
        factor = damping(cuts, lanes, width)
        for f in sequence:
            for copy in circ_copies[f]:
                copy.wait_recv()
            filter_blocks(circles.at[f], filtered.at[f], stack, table, twists, factor)
            if f == 0:
                for copy in home_copies[f]:
                    copy.start()
                continue
            for edge_owner, row, at_pole in ((0, 0, lat == 0), (PARTS - 1, 1, lat == lats - 1)):
                @pl.when(lon == edge_owner)
                def _():
                    for d in range(PARTS):
                        if f == 1:
                            ghost_v_out[d] = filtered[f, d, row : row + 1, :]
                        else:
                            ghost_t_out[d, 0:1, :] = filtered[f, d, row : row + 1, :]
                    if f == 1:
                        for d in range(PARTS):
                            ghost_t_out[d, 1:2, :] = jnp.zeros((1, lanes), jnp.float32)

                        @pl.when(at_pole)
                        def _():
                            for d in range(PARTS):
                                pltpu.make_async_copy(row_out.at[row], pole_in.at[d], pole_recv.at[d]).wait()
                            for d in range(PARTS):
                                ghost_t_out[d, 1:2, :] = pole_in[d, 2:3, :]

            ghost_copies(f - 1, start)
            for copy in home_copies[f]:
                copy.start()

    for copy in edge_copies:
        copy.wait_recv()
    for side, present in ((0, lat > 0), (1, lat < lats - 1)):
        @pl.when(present)
        def _():
            pltpu.make_async_copy(row_out.at[side], row_in.at[side], row_recv.at[side]).wait()

    def with_edges(value, f):
        east, west = edge_in[0][:, f : f + 1], edge_in[1][:, f : f + 1]
        return jnp.where(lane == width, east, jnp.where(lane == lanes - 1, west, value))

    flow, pres = with_edges(raw_g, 2), with_edges(raw_p, 3)

    @pl.when(jnp.logical_not(polar))
    def _():
        smooth[0] = with_edges(raw_u, 0)
        smooth[1] = raw_v
        smooth[2] = with_edges(raw_t, 1)

    def gather(f):
        @pl.when(polar)
        def _():
            for copy in home_copies[f]:
                copy.wait_recv()
            for e in range(PARTS):
                smooth[f, 2 * e : 2 * e + 2, :] = home[f, e]

    poles = (lat == 0, lat == lats - 1)

    def ghosts(g):
        out, into = ((ghost_v_out, ghost_v), (ghost_t_out, ghost_t))[g]
        picked = []
        for side, wanted in ((0, south_filtered), (1, north_filtered)):
            @pl.when(wanted)
            def _():
                pltpu.make_async_copy(out.at[0], into.at[side], ghost_recv.at[g, side]).wait()

            picked.append(jnp.where(wanted, into[side, 0:1, :], row_in[side, g : g + 1, :]))
        return picked

    def merid(f, main, south, north):
        ext[f, 8 : 8 + rows, :] = main
        ext[f, 7:8, :] = south
        ext[f, 8 + rows : 9 + rows, :] = north
        return ext[f, 9 : 9 + rows, :] - ext[f, 7 : 7 + rows, :]

    def zonal(value):
        return pltpu.roll(value, lanes - 1, 1) - pltpu.roll(value, 1, 1)

    gather(1)
    gather(0)
    fu, fv = smooth[0], smooth[1]
    beyond = [jnp.where(poles[side], -g, g) for side, g in enumerate(ghosts(0))]
    bar = scale * zonal(fu) + merid_courant * merid(0, fv, *beyond)
    height[...] = bar
    lev_copies = [
        send(height, heights.at[k], lev_send.at[k], lev_recv.at[k], lev=lax.rem(lev + k, levs))
        for k in range(1, levs)
    ]
    for copy in lev_copies:
        copy.start()
    gather(2)
    ft = smooth[2]
    div = -heat_link_multiplier * ft - pres * (1.0 / levs)
    beyond = []
    for side, g in enumerate(ghosts(1)):
        gp = jnp.where(poles[side], ghost_t[side, 1:2, :], row_in[side, 2:3, :])
        beyond.append(-heat_link_multiplier * g - gp * (1.0 / levs))
    packed[0] = raw_u - coriolis * fv - scale * zonal(div)
    packed[1] = raw_v + coriolis * fu - merid_courant * merid(1, div, *beyond)
    packed[2] = raw_t + bar + scale * zonal(flow * ft)

    for copy in edge_copies:
        copy.wait_send()
    for side in range(2):
        pltpu.make_async_copy(row_out.at[side], row_in.at[side], row_send.at[side]).wait()

    @pl.when(polar)
    def _():
        for copies in circ_copies + home_copies:
            for copy in copies:
                copy.wait_send()

    for g in range(2):
        ghost_copies(g, lambda copy: copy.wait_send())
    total = raw_p + bar
    for copy in lev_copies:
        copy.wait_recv()
    for k in range(1, levs):
        total = total + heights[k]
    packed[3] = total
    for copy in lev_copies:
        copy.wait_send()


def unpack(packed, out_u, out_v, out_t, out_p):
    width = out_p.shape[-1]
    out_u[0] = packed[0, :, :width]
    out_v[0] = packed[1, :, :width]
    out_t[0] = packed[2, :, :width]
    out_p[...] = packed[3, :, :width]


def solution(mesh):
    lats, lons, levs = mesh.shape["lat"], mesh.shape["lon"], mesh.shape["lev"]
    field, plane = P("lev", "lat", "lon"), P("lat", "lon")

    def local(adjoint_u, adjoint_v, adjoint_temp, adjoint_pres, carrying_eastward_flow, cutoff):
        rows, width = adjoint_pres.shape
        lanes = (width + 2 + 127) // 128 * 128
        table, twists = wave_tables(width, lanes)
        sizes = (lats, lons, levs, cutoff.shape[1] // rows)
        vmem = pl.BlockSpec(memory_space=pltpu.VMEM)
        anywhere = pl.BlockSpec(memory_space=pl.ANY)
        f32, dma = jnp.float32, pltpu.SemaphoreType.DMA
        block = (3, PARTS, 2, lanes)
        packed = pl.pallas_call(
            functools.partial(kernel, sizes),
            name="adjoint_step",
            out_shape=pltpu.VMEM((4, rows, lanes), f32),
            in_specs=[anywhere] * 8,
            out_specs=vmem,
            scratch_shapes=[
                pltpu.VMEM((1, rows, width), f32),
                pltpu.VMEM((1, rows, width), f32),
                pltpu.VMEM((1, rows, width), f32),
                pltpu.VMEM((rows, width), f32),
                pltpu.VMEM((1, rows, width), f32),
                pltpu.SMEM(cutoff.shape, jnp.int32),
                pltpu.VMEM(twists.shape, f32),
                pltpu.VMEM(table.shape, jnp.bfloat16),
                pltpu.VMEM((5, rows, lanes), f32),
                pltpu.VMEM(block, f32),
                pltpu.VMEM(block, f32),
                pltpu.VMEM((32, lanes), f32),
                pltpu.VMEM(block, f32),
                pltpu.VMEM(block, f32),
                pltpu.VMEM((3, rows, lanes), f32),
                pltpu.VMEM((2, rows, 128), f32),
                pltpu.VMEM((2, rows, 128), f32),
                pltpu.VMEM((2, 3, lanes), f32),
                pltpu.VMEM((2, 3, lanes), f32),
                pltpu.VMEM((PARTS, 3, lanes), f32),
                pltpu.VMEM((PARTS, 1, lanes), f32),
                pltpu.VMEM((PARTS, 2, lanes), f32),
                pltpu.VMEM((2, 1, lanes), f32),
                pltpu.VMEM((2, 2, lanes), f32),
                pltpu.VMEM((2, rows + 16, lanes), f32),
                pltpu.VMEM((rows, lanes), f32),
                pltpu.VMEM((levs, rows, lanes), f32),
                dma((5,)), dma((3,)), dma((2,)), dma((2,)), dma((2,)), dma((2,)), dma((PARTS,)),
                dma((3, PARTS)), dma((3, PARTS)), dma((3, PARTS)), dma((3, PARTS)),
                dma((2, PARTS)), dma((2, 2)), dma((levs,)), dma((levs,)),
            ],
            compiler_params=pltpu.CompilerParams(collective_id=0, has_side_effects=True),
        )(adjoint_u, adjoint_v, adjoint_temp, adjoint_pres, carrying_eastward_flow, cutoff,
          jnp.asarray(table), jnp.asarray(twists))
        return pl.pallas_call(
            unpack,
            name="hand_on",
            out_shape=[jax.ShapeDtypeStruct(adjoint_u.shape, f32)] * 3
            + [jax.ShapeDtypeStruct(adjoint_pres.shape, f32)],
            in_specs=[vmem],
            out_specs=[vmem] * 4,
        )(pltpu.with_memory_space_constraint(packed, pltpu.VMEM))

    return jax.shard_map(
        local, mesh=mesh, in_specs=(field, field, field, plane, field, P()),
        out_specs=(field, field, field, plane), check_vma=False)
```
